256 devices in a mesh: seq: 32 (over y, x, core), head: 8 (over z).
Axes of the slice: x: 4, y: 4, z: 8, core: 2. Of those that a mesh axis runs over, the one named last changes fastest.
Arguments:
- query_rows: bfloat16 [16384, 4096], P('seq', 'head'), may hold values from -6 to 6
- key_rows: bfloat16 [16384, 4096], P('seq', 'head'), may hold values from -6 to 6
- value_rows: bfloat16 [16384, 4096], P('seq', 'head'), may hold values from -6 to 6
- out_weight: bfloat16 [4096, 4096], P('seq', 'head'), may hold values from -0.09375 to 0.09375
- target_rows: bfloat16 [16384, 4096], P('seq', 'head'), may hold values from -6 to 6
Outputs:
- output: bfloat16 [16384, 4096], P('seq', 'head')
- grad_query: bfloat16 [16384, 4096], P('seq', 'head')
- grad_key: bfloat16 [16384, 4096], P('seq', 'head')
- grad_value: bfloat16 [16384, 4096], P('seq', 'head')
- grad_weight: float32 [4096, 4096], P('seq', 'head')
The draws below stay inside these ranges and needn't reach their ends.
All inputs are finite; a program needn't handle non-finite values.
Results may differ from the reference program's by a relative error of at most 0.019.
Values may be sent and summed in bfloat16 or wider, within the bound.
A program may use at most 64 MiB of HBM per device.

```python
import math
import jax
import jax.numpy as jnp
from jax import lax

D = 4096
H = 32
DH = 128
BLK = 512
TOKENS = 16384
N_HEAD = 8


def spiked(values, own_key, source, target, shards_of, factor):
    owner, partner = [(jnp.arange(values.shape[axis_at]) // (values.shape[axis_at] // shards_of)).reshape([-1 if axis == axis_at else 1 for axis in range(values.ndim)]) for axis_at in (source, target)]
    chosen = jax.random.permutation(own_key, shards_of)[partner]
    strong = (owner == chosen) | (owner == (partner + shards_of // 2) % shards_of)
    return jnp.where(strong, factor * values, values)


def steps_of(rng, shape, shards, low, largest):
    level = 1.0
    for dim, parts in shards:
        steps = jax.random.uniform(jax.random.fold_in(jax.random.fold_in(rng, 6), dim), (parts,), jnp.float32, low / len(shards), largest / len(shards))
        level = level * jnp.repeat(jnp.exp(steps), shape[dim] // parts).reshape((-1,) + (1,) * (len(shape) - 1 - dim))
    return level


def normal_values(rng, shape, width, most, split=(), kind=jnp.bfloat16):
    factor_of = steps_of(rng, shape, split, -0.22, 0.18) if split else 1.0
    result = jax.random.normal(rng, shape, jnp.float32) * width * factor_of
    return jnp.minimum(jnp.maximum(result, -most), most).astype(kind)


def noise_with(key, shape, spread, most, pieces, heavy, held_as=jnp.bfloat16):
    result = spread * jax.random.normal(key, shape, jnp.float32)
    if pieces:
        result = result * steps_of(key, shape, pieces, -0.22, 0.18)
    return jnp.clip(spiked(result, jax.random.fold_in(key, 3), *heavy), -most, most).astype(held_as)


def setup_inputs(seed: int = 0) -> dict:
    key_of = jax.random.split(jax.random.key(seed), 6)
    query_rows = normal_values(key_of[0], (TOKENS, H * DH), 1.0, 6.0, ((0, 32), (1, 8)))
    key_rows = normal_values(key_of[1], (TOKENS, H * DH), 1.0, 6.0, ((0, 32), (1, 8)))
    value_rows = normal_values(key_of[2], (TOKENS, H * DH), 1.0, 6.0, ((0, 32), (1, 8)))
    out_weight = normal_values(key_of[3], (D, H * DH), (H * DH) ** -0.5, 0.09375, ((0, 32), (1, 8)))
    target_rows = noise_with(key_of[4], (TOKENS, D), 1.0, 6.0, ((0, 32), (1, 8)), (0, 1, 32, 2.75))
    return {"query_rows": query_rows, "key_rows": key_rows, "value_rows": value_rows, "out_weight": out_weight, "target_rows": target_rows}


EXACT = lax.Precision.HIGHEST

def reference(query_rows, key_rows, value_rows, out_weight, target_rows):
    block_count = TOKENS // BLK
    positions = jnp.arange(TOKENS, dtype=jnp.float32) + 1.0
    query_scale = lax.rsqrt(jnp.float32(DH) * positions)
    scaled = (query_rows.astype(jnp.float32) * query_scale[:, None]).astype(jnp.bfloat16)
    shaped = (block_count, BLK, H, DH)
    query_blocks = scaled.reshape(shaped)
    key_blocks = key_rows.reshape(shaped)
    value_blocks = value_rows.reshape(shaped)
    causal = jnp.tril(jnp.ones((BLK, BLK), dtype=bool))

    def forward_step(running, inputs):
        queries = inputs[0].astype(jnp.float32)
        keys_now = inputs[1].astype(jnp.float32)
        values_now = inputs[2].astype(jnp.float32)
        inter = jnp.einsum('thd,hde->the', queries, running, precision=EXACT)
        scores = jnp.einsum('thd,shd->hts', queries, keys_now)
        scores = jnp.where(causal, scores, 0.0).astype(jnp.bfloat16)
        intra = jnp.einsum('hts,she->the', scores.astype(jnp.float32), values_now)
        attended_now = (inter + intra).astype(jnp.bfloat16)
        update = jnp.einsum('shd,she->hde', keys_now, values_now)
        return (running + update, (attended_now, running))
    start_state = jnp.zeros((H, DH, DH), jnp.float32)
    final_state, (attended, before) = lax.scan(forward_step, start_state, (query_blocks, key_blocks, value_blocks))
    attended = attended.reshape(TOKENS, H * DH)
    group_width = H * DH // N_HEAD
    grouped_acts = attended.reshape(TOKENS, N_HEAD, group_width).transpose(1, 0, 2)
    grouped_weight = out_weight.reshape(D, N_HEAD, group_width).transpose(1, 0, 2)

    def add_group(running, inputs):
        partial_sum = lax.dot_general(inputs[0], inputs[1], (((1,), (1,)), ((), ())), preferred_element_type=jnp.float32)
        rounded = lax.optimization_barrier(partial_sum.astype(jnp.bfloat16))
        return (running + rounded.astype(jnp.float32), None)
    summed, unused = lax.scan(add_group, jnp.zeros((TOKENS, D), jnp.float32), (grouped_acts, grouped_weight))
    output = summed.astype(jnp.bfloat16)
    residual = (output.astype(jnp.float32) - target_rows.astype(jnp.float32)).astype(jnp.bfloat16)
    grad_attended = jnp.dot(residual, out_weight, preferred_element_type=jnp.float32).astype(jnp.bfloat16)
    grad_weight = lax.dot_general(residual, attended, (((0,), (0,)), ((), ())), preferred_element_type=jnp.float32) * (1.0 / math.sqrt(TOKENS))
    grad_blocks = grad_attended.reshape(shaped)

    def backward_step(running, inputs):
        queries = inputs[0].astype(jnp.float32)
        keys_now = inputs[1].astype(jnp.float32)
        values_now = inputs[2].astype(jnp.float32)
        grads_now = inputs[3].astype(jnp.float32)
        state_now = inputs[4]
        mixed = jnp.einsum('the,she->hts', grads_now, values_now)
        mixed = jnp.where(causal, mixed, 0.0).astype(jnp.bfloat16).astype(jnp.float32)
        scores = jnp.einsum('thd,shd->hts', queries, keys_now)
        scores = jnp.where(causal, scores, 0.0).astype(jnp.bfloat16).astype(jnp.float32)
        grad_scaled = jnp.einsum('the,hde->thd', grads_now, state_now, precision=EXACT)
        grad_scaled = grad_scaled + jnp.einsum('hts,shd->thd', mixed, keys_now)
        key_grad = jnp.einsum('she,hde->shd', values_now, running, precision=EXACT) + jnp.einsum('hts,thd->shd', mixed, queries)
        value_grad = jnp.einsum('shd,hde->she', keys_now, running, precision=EXACT) + jnp.einsum('hts,the->she', scores, grads_now)
        update = jnp.einsum('thd,the->hde', queries, grads_now)
        return (running + update, (grad_scaled, key_grad.astype(jnp.bfloat16), value_grad.astype(jnp.bfloat16)))
    final_grad, (grad_scaled, grad_key, grad_value) = lax.scan(backward_step, start_state, (query_blocks, key_blocks, value_blocks, grad_blocks, before), reverse=True)
    grad_query = (grad_scaled.reshape(TOKENS, H * DH) * query_scale[:, None]).astype(jnp.bfloat16)
    return (output, grad_query, grad_key.reshape(TOKENS, H * DH), grad_value.reshape(TOKENS, H * DH), grad_weight)
```

```python
import math

import jax
import jax.numpy as jnp
from jax import lax
from jax.experimental import pallas as pl
from jax.experimental.pallas import tpu as pltpu
from jax.sharding import Mesh
from jax.sharding import PartitionSpec as P

DH = 128
ROWS = 512
HEADS = 4
SEQ = ("seq_0", "seq_1", "seq_2")
MESH = pl.DeviceIdType.MESH
F32 = jnp.float32
BF16 = jnp.bfloat16
NT = (((1,), (1,)), ((), ()))
NN = (((1,), (0,)), ((), ()))
TN = (((0,), (0,)), ((), ()))
UP_ORDER = (2, 3, 0, 1)
DOWN_ORDER = (0, 1, 2, 3)
GATHER_ORDER = (0, 2, 1, 3)


def dot(a, b, dims):
    return lax.dot_general(a, b, dims, preferred_element_type=F32)


def remote(src, dst, send, recv, **device):
    return pltpu.make_async_remote_copy(
        src_ref=src, dst_ref=dst, send_sem=send, recv_sem=recv, device_id=device, device_id_type=MESH
    )


def wait_bytes(ref, sem):
    pltpu.make_async_copy(ref, ref, sem).wait()


def kernel(
    weight_factor,
    q_in, k_in, v_in, w_in, t_in,
    out_o, gq_o, gk_o, gv_o, gw_o,
    qb, kb, vb, tb, scaled, wf, att, pb, su, sd, ru, rd, res, da, dab, dw, cw, xs, xr, ysend, yown, yrecv,
    scores, gk_acc, gv_acc, oq, ok, ov,
    tot, loc, sib, ct, xrc, rt, yrc, pfs, pfr, px, state,
    in_sem, out_sem, rs_recv, ag_recv, z_send, w_recv, w_send, sc_recv, sc_send, d_recv, d_send,
):
    y = lax.axis_index("seq_0")
    x = lax.axis_index("seq_1")
    c = lax.axis_index("seq_2")
    z = lax.axis_index("head")
    up = lax.rem(z + 1, 8)
    down = lax.rem(z + 7, 8)
    sibling = 1 - c
    half = lax.div(z, 2)
    turn = 2 * lax.rem(z, 2) - 1

    def block(k):
        return lax.rem(z + k + 8, 8)

    def level_row(level):
        shift = {1: 0, 2: turn, 3: -turn, 4: 2}[level]
        return lax.rem(half + shift + 4, 4)

    loads = [
        pltpu.make_async_copy(w_in, wf.at[y, x, c], in_sem.at[0]),
        pltpu.make_async_copy(k_in, kb, in_sem.at[1]),
        pltpu.make_async_copy(v_in, vb, in_sem.at[2]),
        pltpu.make_async_copy(q_in, qb, in_sem.at[3]),
        pltpu.make_async_copy(t_in, tb, in_sem.at[4]),
    ]
    for copy in loads:
        copy.start()

    barrier = pltpu.get_barrier_semaphore()
    partners = [{"head": up}, {"head": down}, {"seq_2": sibling}]
    partners += [{"seq_1": lax.rem(x + d, 4)} for d in (1, 2, 3)]
    partners += [{"seq_0": lax.rem(y + d, 4)} for d in (1, 2, 3)]
    for partner in partners:
        pl.semaphore_signal(barrier, inc=1, device_id=partner, device_id_type=MESH)
    pl.semaphore_wait(barrier, len(partners))

    loads[0].wait()
    for d in (1, 3, 2):
        remote(
            wf.at[y, x, c], wf.at[y, x, c], w_send.at[0], w_recv.at[d - 1], seq_0=lax.rem(y + d, 4)
        ).start()

    def head_columns(h):
        return pl.ds(pl.multiple_of(h * DH, DH), DH)

    def scan_begin(n):
        loc[n] = tot[n].astype(BF16)
        remote(loc.at[n], sib.at[n], sc_send.at[n, 0], sc_recv.at[n, 0], seq_2=sibling).start()

    mine = pl.ds(2 * c, 2)

    def scan_x(n):
        remote(sib.at[n], sib.at[n], sc_send.at[n, 0], sc_recv.at[n, 0], seq_2=sibling).wait_recv()
        chip = tot[n, mine] + sib[n, mine].astype(F32)
        ct[n] = chip.astype(BF16)
        for d in (1, 3, 2):
            remote(
                ct.at[n], xrc.at[n, d - 1], sc_send.at[n, 1], sc_recv.at[n, d], seq_1=lax.rem(x + d, 4)
            ).start()

    def scan_y(n, reverse):
        total = ct[n].astype(F32)
        passed = jnp.zeros((2, DH, DH), F32)
        for d in (1, 3, 2):
            remote(
                ct.at[n], xrc.at[n, d - 1], sc_send.at[n, 1], sc_recv.at[n, d], seq_1=lax.rem(x + d, 4)
            ).wait_recv()
            piece = xrc[n, d - 1].astype(F32)
            total = total + piece
            counts = (d > x) if reverse else (d <= x)
            passed = passed + piece * counts.astype(F32)
        rt[n] = total.astype(BF16)
        px[n] = passed
        for d in (1, 3, 2):
            remote(
                rt.at[n], yrc.at[n, d - 1], sc_send.at[n, 2], sc_recv.at[n, 3 + d], seq_0=lax.rem(y + d, 4)
            ).start()

    def scan_core(n, reverse):
        passed = px[n]
        for d in (1, 3, 2):
            remote(
                rt.at[n], yrc.at[n, d - 1], sc_send.at[n, 2], sc_recv.at[n, 3 + d], seq_0=lax.rem(y + d, 4)
            ).wait_recv()
            counts = (d > y) if reverse else (d <= y)
            passed = passed + yrc[n, d - 1].astype(F32) * counts.astype(F32)
        px[n] = passed
        pfs[n] = passed.astype(BF16)
        remote(pfs.at[n], pfr.at[n], sc_send.at[n, 3], sc_recv.at[n, 7], seq_2=sibling).start()

    def scan_end(n, reverse):
        remote(pfs.at[n], pfr.at[n], sc_send.at[n, 3], sc_recv.at[n, 7], seq_2=sibling).wait_recv()
        own_core = (c == 0) if reverse else (c == 1)
        factor = own_core.astype(F32)
        theirs = pl.ds(2 * sibling, 2)
        state[n, mine] = (px[n] + sib[n, mine].astype(F32) * factor).astype(BF16)
        state[n, theirs] = (pfr[n].astype(F32) + sib[n, theirs].astype(F32) * factor).astype(BF16)

    loads[1].wait()
    loads[2].wait()

    @pl.loop(0, HEADS)
    def _(h):
        cols = head_columns(h)
        tot[0, h] = dot(kb[:, cols], vb[:, cols], TN)

    scan_begin(0)
    first = lax.rem((y * 4 + x) * 2 + c, 32) * ROWS
    positions = (first + lax.broadcasted_iota(jnp.int32, (ROWS, 1), 0) + 1).astype(F32)
    scale = lax.rsqrt(F32(DH) * positions)
    loads[3].wait()
    scaled[...] = (qb[...].astype(F32) * scale).astype(BF16)
    scan_x(0)

    causal = lax.broadcasted_iota(jnp.int32, (ROWS, ROWS), 0) >= lax.broadcasted_iota(
        jnp.int32, (ROWS, ROWS), 1
    )

    for d in (1, 3, 2):
        src = lax.rem(y + 4 - d, 4)
        remote(
            wf.at[src, x, c], wf.at[src, x, c], w_send.at[0], w_recv.at[d - 1], seq_0=lax.rem(y + d, 4)
        ).wait_recv()

    def weight_x(level):
        row = level_row(level)
        for d in (1, 3, 2):
            remote(
                wf.at[row, x, c],
                wf.at[row, x, c],
                w_send.at[1],
                w_recv.at[3 + 3 * (level - 1) + d - 1],
                seq_1=lax.rem(x + d, 4),
            ).start()

    def weight_core(level):
        row = level_row(level)
        for d in (1, 3, 2):
            src = lax.rem(x + 4 - d, 4)
            remote(
                wf.at[row, src, c],
                wf.at[row, src, c],
                w_send.at[1],
                w_recv.at[3 + 3 * (level - 1) + d - 1],
                seq_1=lax.rem(x + d, 4),
            ).wait_recv()
        remote(
            wf.at[row, :, c], wf.at[row, :, c], w_send.at[2], w_recv.at[14 + level], seq_2=sibling
        ).start()

    def weight_ready(level):
        row = level_row(level)
        remote(
            wf.at[row, :, sibling], wf.at[row, :, sibling], w_send.at[2], w_recv.at[14 + level], seq_2=sibling
        ).wait_recv()

    for level in (4, 3, 2, 1):
        weight_x(level)

    @pl.loop(0, HEADS)
    def _(h):
        cols = head_columns(h)
        s = dot(scaled[:, cols], kb[:, cols], NT)
        scores[h] = jnp.where(causal, s, 0.0).astype(BF16)

    scan_y(0, False)

    @pl.loop(0, HEADS)
    def _(h):
        cols = head_columns(h)
        gk_acc[:, cols] = dot(scores[h], vb[:, cols], NN)

    weight_core(4)
    scan_core(0, False)
    scan_end(0, False)

    @pl.loop(0, HEADS)
    def _(h):
        cols = head_columns(h)
        att[:, cols] = (dot(scaled[:, cols], state[0, h], NN) + gk_acc[:, cols]).astype(BF16)

    def weight_block(b):
        w = wf[lax.div(b, 2), pl.ds(2 * lax.rem(b, 2), 2)]
        return w.reshape(ROWS, ROWS)

    def partial(u, b):
        pb[u] = dot(att[...], weight_block(b), NT).reshape(4, 128, ROWS)

    def reduce_copy(u, idx):
        src, dst = (su, ru) if u == 0 else (sd, rd)
        return remote(
            src.at[idx], dst.at[idx], z_send.at[u], rs_recv.at[u, idx], head=up if u == 0 else down
        )

    def reduce_send(u, idx, r, received):
        src, dst = (su, ru) if u == 0 else (sd, rd)
        value = pb[u, r]
        if received is not None:
            reduce_copy(u, received).wait_recv()
            value = value + dst[received].astype(F32)
        src[idx] = value.astype(BF16)
        reduce_copy(u, idx).start()

    weight_ready(4)
    partial(0, block(4))
    pb[1] = pb[0]
    for i in (0, 1):
        reduce_send(0, i, i, None)
        reduce_send(1, i, 2 + i, None)
    weight_core(3)
    weight_ready(3)
    partial(0, block(3))
    partial(1, block(-3))
    for j in range(4):
        reduce_send(0, 2 + j, UP_ORDER[j], None if j < 2 else j - 2)
        reduce_send(1, 2 + j, DOWN_ORDER[j], None if j < 2 else j - 2)
    for k in (2, 1):
        weight_core(k)
        weight_ready(k)
        partial(0, block(k))
        partial(1, block(-k))
        for j in range(4):
            idx = 4 * (3 - k) + 2 + j
            reduce_send(0, idx, UP_ORDER[j], idx - 4)
            reduce_send(1, idx, DOWN_ORDER[j], idx - 4)
    partial(0, z)

    def gather_copy(u, idx, b, r):
        return remote(
            res.at[b, r], res.at[b, r], z_send.at[2 + u], ag_recv.at[u, idx], head=up if u == 0 else down
        )

    loads[4].wait()
    for j, r in enumerate(GATHER_ORDER):
        i_up = 10 + UP_ORDER.index(r)
        i_down = 10 + DOWN_ORDER.index(r)
        reduce_copy(0, i_up).wait_recv()
        reduce_copy(1, i_down).wait_recv()
        value = (pb[0, r] + ru[i_up].astype(F32) + rd[i_down].astype(F32)).astype(BF16)
        rows = pl.ds(r * 128, 128)
        ov[rows, :] = value
        res[z, r] = (value.astype(F32) - tb[rows, :].astype(F32)).astype(BF16)
        gather_copy(0, j, z, r).start()
        gather_copy(1, j, z, r).start()
    out_copy = pltpu.make_async_copy(ov, out_o, out_sem.at[0])
    out_copy.start()

    def grads(b, begin=False):
        r_b = res[b].reshape(ROWS, ROWS)
        term = dot(r_b, weight_block(b), NN)
        da[...] = term if begin else da[...] + term

    def weight_grads(b):
        r_b = res[b].reshape(ROWS, ROWS)
        d_b = dot(r_b, att[...], TN).astype(BF16)
        dw[lax.div(b, 2), pl.ds(2 * lax.rem(b, 2), 2)] = d_b.reshape(2, 2, 128, ROWS)

    def dw_core(level):
        row = level_row(level)
        remote(
            dw.at[row, :, sibling], cw.at[level - 1], d_send.at[0], d_recv.at[level - 1], seq_2=sibling
        ).start()

    def dw_x(level):
        row = level_row(level)
        remote(
            cw.at[level - 1], cw.at[level - 1], d_send.at[0], d_recv.at[level - 1], seq_2=sibling
        ).wait_recv()
        for d in (1, 3, 2, 0):
            to = lax.rem(x + d, 4)
            xs[level - 1, to] = (
                dw[row, to, c].astype(F32) + cw[level - 1, to].astype(F32)
            ).astype(BF16)
            if d:
                remote(
                    xs.at[level - 1, to],
                    xr.at[level - 1, d - 1],
                    d_send.at[1],
                    d_recv.at[4 + 3 * (level - 1) + d - 1],
                    seq_1=to,
                ).start()

    def dw_y(level):
        row = level_row(level)
        total = xs[level - 1, x].astype(F32)
        for d in (1, 3, 2):
            remote(
                xr.at[level - 1, d - 1],
                xr.at[level - 1, d - 1],
                d_send.at[1],
                d_recv.at[4 + 3 * (level - 1) + d - 1],
                seq_1=lax.rem(x + d, 4),
            ).wait_recv()
            total = total + xr[level - 1, d - 1].astype(F32)

        @pl.when(row == y)
        def _():
            yown[...] = total

        @pl.when(row != y)
        def _():
            ysend[level - 1] = total.astype(BF16)
            d = lax.rem(row - y + 4, 4)
            remote(
                ysend.at[level - 1], yrecv.at[d - 1], d_send.at[2], d_recv.at[16 + d - 1], seq_0=row
            ).start()

    grads(z, begin=True)
    weight_grads(z)
    for k in (1, 2, 3):
        for j, r in enumerate(GATHER_ORDER):
            for u in (0, 1):
                b = block(-k if u == 0 else k)
                gather_copy(u, 4 * (k - 1) + j, b, r).wait_recv()
                if k < 3:
                    gather_copy(u, 4 * k + j, b, r).start()
                elif u == 0 and j < 2:
                    gather_copy(u, 12 + j, b, r).start()
                elif u == 1 and j >= 2:
                    gather_copy(u, 12 + j - 2, b, r).start()

        @pl.loop(0, 2)
        def _(u, k=k):
            b = block(k * (2 * u - 1))
            grads(b)
            weight_grads(b)

        dw_core(k)
        if k >= 2:
            dw_x(k - 1)
        if k >= 3:
            dw_y(k - 2)

    b4 = block(4)
    for i in (0, 1):
        gather_copy(0, 12 + i, b4, GATHER_ORDER[i]).wait_recv()
        gather_copy(1, 12 + i, b4, GATHER_ORDER[2 + i]).wait_recv()
    grads(b4)
    dab[...] = da[...].astype(BF16)

    @pl.loop(0, HEADS)
    def _(h):
        cols = head_columns(h)
        tot[1, h] = dot(scaled[:, cols], dab[:, cols], TN)

    scan_begin(1)
    weight_grads(b4)
    dw_core(4)
    scan_x(1)
    dw_x(3)
    dw_x(4)

    @pl.loop(0, HEADS)
    def _(h):
        cols = head_columns(h)
        mixed = jnp.where(causal, dot(dab[:, cols], vb[:, cols], NT), 0.0).astype(BF16)
        g = dot(dab[:, cols], state[0, h], NT) + dot(mixed, kb[:, cols], NN)
        oq[:, cols] = (g * scale).astype(BF16)
        gk_acc[:, cols] = dot(mixed, scaled[:, cols], TN)
        gv_acc[:, cols] = dot(scores[h], dab[:, cols], TN)

    scan_y(1, True)
    q_copy = pltpu.make_async_copy(oq, gq_o, out_sem.at[1])
    q_copy.start()
    dw_y(2)
    dw_y(3)
    scan_core(1, True)
    dw_y(4)
    scan_end(1, True)
    out_copy.wait()

    @pl.loop(0, HEADS)
    def _(h):
        cols = head_columns(h)
        ok[:, cols] = (gk_acc[:, cols] + dot(vb[:, cols], state[1, h], NT)).astype(BF16)
        ov[:, cols] = (gv_acc[:, cols] + dot(kb[:, cols], state[1, h], NN)).astype(BF16)

    k_copy = pltpu.make_async_copy(ok, gk_o, out_sem.at[2])
    k_copy.start()
    v_copy = pltpu.make_async_copy(ov, gv_o, out_sem.at[3])
    v_copy.start()
    total = yown[...]
    for d in (1, 3, 2):
        remote(
            yrecv.at[d - 1], yrecv.at[d - 1], d_send.at[2], d_recv.at[16 + d - 1], seq_0=lax.rem(y + d, 4)
        ).wait_recv()
        total = total + yrecv[d - 1].astype(F32)
    yown[...] = total * weight_factor
    w_copy = pltpu.make_async_copy(yown, gw_o, out_sem.at[4])
    w_copy.start()

    wait_bytes(su, z_send.at[0])
    wait_bytes(sd, z_send.at[1])
    wait_bytes(su, z_send.at[2])
    wait_bytes(sd, z_send.at[3])
    wait_bytes(xr.at[0], w_send.at[0])
    wait_bytes(xr, w_send.at[1])
    wait_bytes(xs, w_send.at[2])
    wait_bytes(cw, d_send.at[0])
    wait_bytes(xr, d_send.at[1])
    wait_bytes(yrecv, d_send.at[2])
    for n in (0, 1):
        wait_bytes(loc.at[n], sc_send.at[n, 0])
        wait_bytes(xrc.at[n], sc_send.at[n, 1])
        wait_bytes(yrc.at[n], sc_send.at[n, 2])
        wait_bytes(pfs.at[n], sc_send.at[n, 3])
    for copy in (q_copy, k_copy, v_copy, w_copy):
        copy.wait()


def on_device(query_rows, key_rows, value_rows, out_weight, target_rows):
    rows = jax.ShapeDtypeStruct((ROWS, ROWS), BF16)
    total_rows = query_rows.shape[0] * lax.axis_size(SEQ)
    full = (ROWS, ROWS)
    vm = pltpu.VMEM
    scratch = (
        [vm(full, BF16)] * 5
        + [
            vm((4, 4, 2, 128, ROWS), BF16),
            vm(full, BF16),
            vm((2, 4, 128, ROWS), F32),
        ]
        + [vm((14, 128, ROWS), BF16)] * 4
        + [
            vm((8, 4, 128, ROWS), BF16),
            vm(full, F32),
            vm(full, BF16),
            vm((4, 4, 2, 128, ROWS), BF16),
            vm((4, 4, 128, ROWS), BF16),
            vm((4, 4, 128, ROWS), BF16),
            vm((4, 3, 128, ROWS), BF16),
            vm((4, 128, ROWS), BF16),
            vm((128, ROWS), F32),
            vm((3, 128, ROWS), BF16),
            vm((HEADS, ROWS, ROWS), BF16),
            vm(full, F32),
            vm(full, F32),
        ]
        + [vm(full, BF16)] * 3
        + [
            vm((2, HEADS, DH, DH), F32),
            vm((2, HEADS, DH, DH), BF16),
            vm((2, HEADS, DH, DH), BF16),
            vm((2, 2, DH, DH), BF16),
            vm((2, 3, 2, DH, DH), BF16),
            vm((2, 2, DH, DH), BF16),
            vm((2, 3, 2, DH, DH), BF16),
            vm((2, 2, DH, DH), BF16),
            vm((2, 2, DH, DH), BF16),
            vm((2, 2, DH, DH), F32),
            vm((2, HEADS, DH, DH), BF16),
        ]
    )
    dma = pltpu.SemaphoreType.DMA
    scratch += [
        dma((5,)), dma((5,)), dma((2, 14)), dma((2, 14)), dma((4,)), dma((19,)), dma((3,)),
        dma((2, 8)), dma((2, 4)), dma((19,)), dma((3,)),
    ]
    anywhere = pl.BlockSpec(memory_space=pl.ANY)

    def body(*refs):
        kernel(1.0 / math.sqrt(total_rows), *refs)

    return pl.pallas_call(
        body,
        out_shape=(rows, rows, rows, rows, jax.ShapeDtypeStruct((128, ROWS), F32)),
        in_specs=[anywhere] * 5,
        out_specs=(anywhere,) * 5,
        scratch_shapes=scratch,
        compiler_params=pltpu.CompilerParams(
            collective_id=0, has_side_effects=True, vmem_limit_bytes=60 * 1024 * 1024
        ),
        name="linear_attention",
    )(query_rows, key_rows, value_rows, out_weight, target_rows)


def solution(mesh):
    torus = Mesh(
        mesh.devices.reshape(4, 4, 2, mesh.shape["head"]), ("seq_0", "seq_1", "seq_2", "head")
    )
    spec = P(SEQ, "head")
    return jax.shard_map(
        on_device, mesh=torus, in_specs=(spec,) * 5, out_specs=(spec,) * 5, check_vma=False
    )
```

```python
import math

import jax
import jax.numpy as jnp
from jax import lax
from jax.experimental import pallas as pl
from jax.experimental.pallas import tpu as pltpu
from jax.sharding import Mesh
from jax.sharding import PartitionSpec as P

DH = 128
ROWS = 512
HEADS = 4
SEQ = ("seq_0", "seq_1", "seq_2")
MESH = pl.DeviceIdType.MESH
F32 = jnp.float32
BF16 = jnp.bfloat16
NT = (((1,), (1,)), ((), ()))
NN = (((1,), (0,)), ((), ()))
TN = (((0,), (0,)), ((), ()))


def dot(a, b, dims):
    return lax.dot_general(a, b, dims, preferred_element_type=F32)


def remote(src, dst, send, recv, **device):
    return pltpu.make_async_remote_copy(
        src_ref=src, dst_ref=dst, send_sem=send, recv_sem=recv, device_id=device, device_id_type=MESH
    )


def wait_bytes(ref, sem):
    pltpu.make_async_copy(ref, ref, sem).wait()


def kernel(
    weight_factor,
    q_in, k_in, v_in, w_in, t_in,
    out_o, gq_o, gk_o, gv_o, gw_o,
    qb, kb, vb, tb, scaled, wf, att, pb, su, sd, ru, rd, res, da, dab, dw, cw, xs, xh, xr, ysend, yown, yrecv,
    scores, gk_acc, gv_acc, oq, ok, ov,
    tot, loc, sib, ct, xrc, rt, yrc, pfs, pfr, px, state,
    in_sem, out_sem, rs_recv, ag_recv, z_send, wy_recv, wx_recv, wc_recv, w_send, sc_recv, sc_send,
    dc_recv, dx_recv, dy_recv, d_send,
):
    y = lax.axis_index("seq_0")
    x = lax.axis_index("seq_1")
    c = lax.axis_index("seq_2")
    z = lax.axis_index("head")
    up = lax.rem(z + 1, 8)
    down = lax.rem(z + 7, 8)
    sibling = 1 - c
    right = lax.rem(x + 1, 4)
    left = lax.rem(x + 3, 4)
    across = lax.rem(x + 2, 4)
    half = lax.div(z, 2)
    turn = 2 * lax.rem(z, 2) - 1
    first_half = pl.ds(0, 64)
    second_half = pl.ds(64, 64)

    def block(k):
        return lax.rem(z + k + 8, 8)

    def level_row(level):
        shift = {1: 0, 2: turn, 3: -turn, 4: 2}[level]
        return lax.rem(half + shift + 4, 4)

    loads = [
        pltpu.make_async_copy(w_in, wf.at[y, x, c], in_sem.at[0]),
        pltpu.make_async_copy(k_in, kb, in_sem.at[1]),
        pltpu.make_async_copy(v_in, vb, in_sem.at[2]),
        pltpu.make_async_copy(q_in, qb, in_sem.at[3]),
        pltpu.make_async_copy(t_in, tb, in_sem.at[4]),
    ]
    for copy in loads:
        copy.start()

    barrier = pltpu.get_barrier_semaphore()
    partners = [{"head": up}, {"head": down}, {"seq_2": sibling}]
    partners += [{"seq_1": lax.rem(x + d, 4)} for d in (1, 2, 3)]
    partners += [{"seq_0": lax.rem(y + d, 4)} for d in (1, 2, 3)]
    for partner in partners:
        pl.semaphore_signal(barrier, inc=1, device_id=partner, device_id_type=MESH)
    pl.semaphore_wait(barrier, len(partners))

    def weight_y():
        for d in (2, 3, 1):
            remote(
                wf.at[y, x, c], wf.at[y, x, c], w_send.at[0], wy_recv.at[d - 1], seq_0=lax.rem(y + d, 4)
            ).start()

    def weight_to_core(row, col, slot):
        return remote(
            wf.at[row, col, c], wf.at[row, col, c], w_send.at[2], wc_recv.at[slot], seq_2=sibling
        )

    def weight_side(level, toward_right, whole):
        row = level_row(level)
        to, source = (right, left) if toward_right else (left, right)
        slot = 4 * (level - 1) + (0 if toward_right else 1) + (0 if whole else 2)
        sem = wx_recv.at[slot]
        if whole:
            sent, got = wf.at[row, x, c], wf.at[row, source, c]
        else:
            part = first_half if toward_right else second_half
            sent, got = wf.at[row, source, c, part], wf.at[row, across, c, part]
        return (
            lambda: remote(sent, sent, w_send.at[1], sem, seq_1=to).start(),
            lambda: remote(got, got, w_send.at[1], sem, seq_1=to).wait_recv(),
        )

    def weight_1(level):
        row = level_row(level)

        @pl.when(row != y)
        def _():
            d = lax.rem(y - row + 4, 4)
            remote(
                wf.at[row, x, c], wf.at[row, x, c], w_send.at[0], wy_recv.at[d - 1], seq_0=row
            ).wait_recv()

        weight_side(level, True, True)[0]()
        weight_side(level, False, True)[0]()
        weight_to_core(row, x, 4 * (level - 1)).start()

    def weight_2(level):
        row = level_row(level)
        for i, toward_right in enumerate((True, False)):
            weight_side(level, toward_right, True)[1]()
            weight_side(level, toward_right, False)[0]()
            weight_to_core(row, left if toward_right else right, 4 * (level - 1) + 1 + i).start()

    def weight_3(level):
        row = level_row(level)
        for toward_right in (True, False):
            weight_side(level, toward_right, False)[1]()
        weight_to_core(row, across, 4 * (level - 1) + 3).start()

    def weight_ready(level):
        row = level_row(level)
        for i, col in enumerate((x, left, right, across)):
            slot = 4 * (level - 1) + i
            remote(
                wf.at[row, col, sibling], wf.at[row, col, sibling], w_send.at[2], wc_recv.at[slot],
                seq_2=sibling,
            ).wait_recv()

    loads[0].wait()

    @pl.when(level_row(4) == y)
    def _():
        weight_y()

    def head_columns(h):
        return pl.ds(pl.multiple_of(h * DH, DH), DH)

    def scan_begin(n):
        loc[n] = tot[n].astype(BF16)
        remote(loc.at[n], sib.at[n], sc_send.at[n, 0], sc_recv.at[n, 0], seq_2=sibling).start()

    mine = pl.ds(2 * c, 2)

    def scan_x(n):
        remote(sib.at[n], sib.at[n], sc_send.at[n, 0], sc_recv.at[n, 0], seq_2=sibling).wait_recv()
        chip = tot[n, mine] + sib[n, mine].astype(F32)
        ct[n] = chip.astype(BF16)
        for d in (2, 1, 3):
            remote(
                ct.at[n], xrc.at[n, d - 1], sc_send.at[n, 1], sc_recv.at[n, d], seq_1=lax.rem(x + d, 4)
            ).start()

    def scan_y(n, reverse):
        total = ct[n].astype(F32)
        passed = jnp.zeros((2, DH, DH), F32)
        for d in (1, 3, 2):
            remote(
                ct.at[n], xrc.at[n, d - 1], sc_send.at[n, 1], sc_recv.at[n, d], seq_1=lax.rem(x + d, 4)
            ).wait_recv()
            piece = xrc[n, d - 1].astype(F32)
            total = total + piece
            counts = (d > x) if reverse else (d <= x)
            passed = passed + piece * counts.astype(F32)
        rt[n] = total.astype(BF16)
        px[n] = passed
        for d in (2, 1, 3):
            remote(
                rt.at[n], yrc.at[n, d - 1], sc_send.at[n, 2], sc_recv.at[n, 3 + d], seq_0=lax.rem(y + d, 4)
            ).start()

    def scan_core(n, reverse):
        passed = px[n]
        for d in (1, 3, 2):
            remote(
                rt.at[n], yrc.at[n, d - 1], sc_send.at[n, 2], sc_recv.at[n, 3 + d], seq_0=lax.rem(y + d, 4)
            ).wait_recv()
            counts = (d > y) if reverse else (d <= y)
            passed = passed + yrc[n, d - 1].astype(F32) * counts.astype(F32)
        px[n] = passed
        pfs[n] = passed.astype(BF16)
        remote(pfs.at[n], pfr.at[n], sc_send.at[n, 3], sc_recv.at[n, 7], seq_2=sibling).start()

    def scan_end(n, reverse):
        remote(pfs.at[n], pfr.at[n], sc_send.at[n, 3], sc_recv.at[n, 7], seq_2=sibling).wait_recv()
        own_core = (c == 0) if reverse else (c == 1)
        factor = own_core.astype(F32)
        theirs = pl.ds(2 * sibling, 2)
        state[n, mine] = (px[n] + sib[n, mine].astype(F32) * factor).astype(BF16)
        state[n, theirs] = (pfr[n].astype(F32) + sib[n, theirs].astype(F32) * factor).astype(BF16)

    loads[1].wait()
    loads[2].wait()

    @pl.loop(0, HEADS)
    def _(h):
        cols = head_columns(h)
        tot[0, h] = dot(kb[:, cols], vb[:, cols], TN)

    scan_begin(0)

    @pl.when(level_row(3) == y)
    def _():
        weight_y()

    first = lax.rem((y * 4 + x) * 2 + c, 32) * ROWS
    positions = (first + lax.broadcasted_iota(jnp.int32, (ROWS, 1), 0) + 1).astype(F32)
    scale = lax.rsqrt(F32(DH) * positions)
    loads[3].wait()
    scaled[...] = (qb[...].astype(F32) * scale).astype(BF16)
    scan_x(0)

    causal = lax.broadcasted_iota(jnp.int32, (ROWS, ROWS), 0) >= lax.broadcasted_iota(
        jnp.int32, (ROWS, ROWS), 1
    )

    @pl.loop(0, HEADS)
    def _(h):
        cols = head_columns(h)
        s = dot(scaled[:, cols], kb[:, cols], NT)
        scores[h] = jnp.where(causal, s, 0.0).astype(BF16)

    weight_1(4)

    @pl.loop(0, HEADS)
    def _(h):
        cols = head_columns(h)
        gk_acc[:, cols] = dot(scores[h], vb[:, cols], NN)

    scan_y(0, False)

    @pl.when(jnp.logical_and(level_row(4) != y, level_row(3) != y))
    def _():
        weight_y()

    weight_2(4)
    weight_1(3)
    scan_core(0, False)
    weight_3(4)
    scan_end(0, False)

    @pl.loop(0, HEADS)
    def _(h):
        cols = head_columns(h)
        att[:, cols] = (dot(scaled[:, cols], state[0, h], NN) + gk_acc[:, cols]).astype(BF16)

    up_order = (2 + c, 3 - c, c, 1 - c)
    down_order = (c, 1 - c, 2 + c, 3 - c)
    gather_order = (c, 2 + c, 1 - c, 3 - c)

    def block_cols(b):
        return lax.div(b, 2), pl.ds(2 * lax.rem(b, 2), 2)

    def weight_block(b):
        row, cols = block_cols(b)
        return wf[row, cols].reshape(ROWS, ROWS)

    def partial(u, b):
        value = dot(att[...], weight_block(b), NT)
        for r in range(4):
            pb[u, r] = value[:, r * 128 : (r + 1) * 128]

    def reduce_copy(u, idx):
        src, dst = (su, ru) if u == 0 else (sd, rd)
        return remote(
            src.at[idx], dst.at[idx], z_send.at[u], rs_recv.at[u, idx], head=up if u == 0 else down
        )

    def reduce_send(u, idx, r, received):
        src, dst = (su, ru) if u == 0 else (sd, rd)
        value = pb[u, r]
        if received is not None:
            reduce_copy(u, received).wait_recv()
            value = value + dst[received].astype(F32)
        src[idx] = value.astype(BF16)
        reduce_copy(u, idx).start()

    row4, cols4 = block_cols(block(4))
    for i, core in enumerate((c, sibling)):
        if i == 1:
            weight_ready(4)
        value = dot(att[...], wf[row4, cols4, core].reshape(256, ROWS), NT)
        su[i] = value[:, 0:128].astype(BF16)
        sd[i] = value[:, 128:256].astype(BF16)
        reduce_copy(0, i).start()
        reduce_copy(1, i).start()
    weight_2(3)
    weight_1(2)
    weight_3(3)
    weight_ready(3)
    partial(0, block(3))
    partial(1, block(-3))
    for j in range(4):
        reduce_send(0, 2 + j, up_order[j], None if j < 2 else j - 2)
        reduce_send(1, 2 + j, down_order[j], None if j < 2 else j - 2)
    for k in (2, 1):
        weight_2(k)
        if k == 2:
            weight_1(1)
        weight_3(k)
        weight_ready(k)
        partial(0, block(k))
        partial(1, block(-k))
        for j in range(4):
            idx = 4 * (3 - k) + 2 + j
            reduce_send(0, idx, up_order[j], idx - 4)
            reduce_send(1, idx, down_order[j], idx - 4)
    partial(0, z)

    def gather_copy(u, idx, b, r):
        return remote(
            res.at[b, r], res.at[b, r], z_send.at[2 + u], ag_recv.at[u, idx], head=up if u == 0 else down
        )

    loads[4].wait()
    for j, r in enumerate(gather_order):
        i_up = 10 + (2, 0, 3, 1)[j]
        i_down = 10 + (0, 2, 1, 3)[j]
        reduce_copy(0, i_up).wait_recv()
        reduce_copy(1, i_down).wait_recv()
        value = (pb[0, r] + ru[i_up].astype(F32) + rd[i_down].astype(F32)).astype(BF16)
        cols = pl.ds(pl.multiple_of(r * 128, 128), 128)
        ov[:, cols] = value
        res[z, r] = (value.astype(F32) - tb[:, cols].astype(F32)).astype(BF16)
        gather_copy(0, j, z, r).start()
        gather_copy(1, j, z, r).start()
    out_copy = pltpu.make_async_copy(ov, out_o, out_sem.at[0])
    out_copy.start()

    def residual_block(b, pieces):
        return jnp.concatenate([res[b, r] for r in pieces], axis=1)

    def grads(b, begin=False):
        term = dot(residual_block(b, range(4)), weight_block(b), NN)
        da[...] = term if begin else da[...] + term

    def weight_grads(b):
        row, cols = block_cols(b)
        d_b = dot(residual_block(b, range(4)), att[...], TN).astype(BF16)
        dw[row, cols] = d_b.reshape(2, 2, 128, ROWS)

    def dw_to_core(row, cols, level, slot):
        return remote(
            dw.at[row, cols, sibling], cw.at[level - 1, cols], d_send.at[0], dc_recv.at[slot], seq_2=sibling
        )

    every = pl.ds(0, 4)

    def dw_side(level, toward_right, whole):
        to = right if toward_right else left
        side = 0 if toward_right else 1
        sem = dx_recv.at[4 * (level - 1) + side + (0 if whole else 2)]
        if whole:
            return remote(xs.at[level - 1, to], xr.at[level - 1, side], d_send.at[1], sem, seq_1=to)
        part = first_half if toward_right else second_half
        return remote(
            xs.at[level - 1, across, part], xh.at[level - 1, side], d_send.at[1], sem, seq_1=to
        )

    def dw_1(level):
        row = level_row(level)
        if level < 4:
            dw_to_core(row, every, level, level - 1).wait_recv()
        else:
            dw_to_core(row, other_cols, level, 3).wait_recv()
            dw_to_core(row, pl.ds(first_col, 1), level, 4).wait_recv()
            dw_to_core(row, pl.ds(first_col + 1, 1), level, 5).wait_recv()
        for i, to in enumerate((across, right, left, x)):
            xs[level - 1, to] = (
                dw[row, to, c].astype(F32) + cw[level - 1, to].astype(F32)
            ).astype(BF16)
            if i == 0:
                dw_side(level, True, False).start()
                dw_side(level, False, False).start()

    def dw_2(level):
        for side, toward_right in enumerate((True, False)):
            to = right if toward_right else left
            part = first_half if toward_right else second_half
            dw_side(level, toward_right, False).wait_recv()
            value = xs[level - 1, to, part].astype(F32) + xh[level - 1, side].astype(F32)
            xs[level - 1, to, part] = value.astype(BF16)
            dw_side(level, toward_right, True).start()

    def dw_3(level):
        row = level_row(level)
        total = xs[level - 1, x].astype(F32)
        for side, toward_right in enumerate((True, False)):
            dw_side(level, toward_right, True).wait_recv()
            total = total + xr[level - 1, side].astype(F32)

        @pl.when(row == y)
        def _():
            yown[...] = total

        @pl.when(row != y)
        def _():
            ysend[level - 1] = total.astype(BF16)
            d = lax.rem(row - y + 4, 4)
            remote(
                ysend.at[level - 1], yrecv.at[d - 1], d_send.at[2], dy_recv.at[d - 1], seq_0=row
            ).start()

    first_col = 2 * lax.rem(block(4), 2)
    other_cols = pl.ds(2 - first_col, 2)

    grads(z, begin=True)
    weight_grads(z)
    for k in (1, 2, 3):
        for j, r in enumerate(gather_order):
            for u in (0, 1):
                b = block(-k if u == 0 else k)
                gather_copy(u, 4 * (k - 1) + j, b, r).wait_recv()
                if k < 3:
                    gather_copy(u, 4 * k + j, b, r).start()
                elif u == 0 and j < 2:
                    gather_copy(u, 12 + j, b, r).start()
                elif u == 1 and j >= 2:
                    gather_copy(u, 12 + j - 2, b, r).start()
            if k >= 2 and j == 0:
                dw_1(k - 1)
            if k >= 2 and j == 2:
                dw_2(k - 1)
            if k >= 3 and j == 1:
                dw_3(k - 2)

        @pl.loop(0, 2)
        def _(u, k=k):
            b = block(k * (2 * u - 1))
            grads(b)
            weight_grads(b)

        dw_to_core(level_row(k), every, k, k - 1).start()

    dw_to_core(level_row(4), other_cols, 4, 3).start()
    dw_3(2)
    dw_1(3)

    b4 = block(4)

    def last_half(i):
        col = first_col + i
        gather_copy(0, 12 + i, b4, gather_order[i]).wait_recv()
        gather_copy(1, 12 + i, b4, gather_order[2 + i]).wait_recv()
        term = dot(residual_block(b4, (2 * i, 2 * i + 1)), wf[row4, col].reshape(256, ROWS), NN)
        if i == 0:
            da[...] += term
        else:
            dab[...] = (da[...] + term).astype(BF16)

    def last_weight_half(i):
        col = first_col + i
        d_b = dot(residual_block(b4, (2 * i, 2 * i + 1)), att[...], TN).astype(BF16)
        dw[row4, col] = d_b.reshape(2, 128, ROWS)
        dw_to_core(row4, pl.ds(col, 1), 4, 4 + i).start()

    last_half(0)
    last_weight_half(0)
    dw_2(3)
    last_half(1)

    @pl.loop(0, HEADS)
    def _(h):
        cols = head_columns(h)
        tot[1, h] = dot(scaled[:, cols], dab[:, cols], TN)

    scan_begin(1)
    last_weight_half(1)
    scan_x(1)
    dw_1(4)
    dw_3(3)

    def gradient_pair(start):
        @pl.loop(start, start + 2)
        def _(h):
            cols = head_columns(h)
            mixed = jnp.where(causal, dot(dab[:, cols], vb[:, cols], NT), 0.0).astype(BF16)
            g = dot(dab[:, cols], state[0, h], NT) + dot(mixed, kb[:, cols], NN)
            oq[:, cols] = (g * scale).astype(BF16)
            gk_acc[:, cols] = dot(mixed, scaled[:, cols], TN)
            gv_acc[:, cols] = dot(scores[h], dab[:, cols], TN)

    gradient_pair(0)
    dw_2(4)
    gradient_pair(2)
    scan_y(1, True)
    q_copy = pltpu.make_async_copy(oq, gq_o, out_sem.at[1])
    q_copy.start()
    dw_3(4)
    scan_core(1, True)
    scan_end(1, True)
    out_copy.wait()

    @pl.loop(0, HEADS)
    def _(h):
        cols = head_columns(h)
        ok[:, cols] = (gk_acc[:, cols] + dot(vb[:, cols], state[1, h], NT)).astype(BF16)
        ov[:, cols] = (gv_acc[:, cols] + dot(kb[:, cols], state[1, h], NN)).astype(BF16)

    k_copy = pltpu.make_async_copy(ok, gk_o, out_sem.at[2])
    k_copy.start()
    v_copy = pltpu.make_async_copy(ov, gv_o, out_sem.at[3])
    v_copy.start()
    total = yown[...]
    for d in (1, 3, 2):
        remote(
            yrecv.at[d - 1], yrecv.at[d - 1], d_send.at[2], dy_recv.at[d - 1], seq_0=lax.rem(y + d, 4)
        ).wait_recv()
        total = total + yrecv[d - 1].astype(F32)
    yown[...] = total * weight_factor
    w_copy = pltpu.make_async_copy(yown, gw_o, out_sem.at[4])
    w_copy.start()

    wait_bytes(su, z_send.at[0])
    wait_bytes(sd, z_send.at[1])
    wait_bytes(su, z_send.at[2])
    wait_bytes(sd, z_send.at[3])
    wait_bytes(yrecv, w_send.at[0])
    wait_bytes(su.at[pl.ds(0, 12)], w_send.at[1])
    wait_bytes(xs, w_send.at[2])
    wait_bytes(cw, d_send.at[0])
    wait_bytes(su.at[pl.ds(0, 12)], d_send.at[1])
    wait_bytes(yrecv, d_send.at[2])
    for n in (0, 1):
        wait_bytes(loc.at[n], sc_send.at[n, 0])
        wait_bytes(xrc.at[n], sc_send.at[n, 1])
        wait_bytes(yrc.at[n], sc_send.at[n, 2])
        wait_bytes(pfs.at[n], sc_send.at[n, 3])
    for copy in (q_copy, k_copy, v_copy, w_copy):
        copy.wait()


def write_out(*refs):
    sems = refs[-1]
    copies = [pltpu.make_async_copy(refs[i], refs[5 + i], sems.at[i]) for i in range(5)]
    for copy in copies:
        copy.start()
    for copy in copies:
        copy.wait()


def on_device(query_rows, key_rows, value_rows, out_weight, target_rows):
    rows = jax.ShapeDtypeStruct((ROWS, ROWS), BF16)
    total_rows = query_rows.shape[0] * lax.axis_size(SEQ)
    full = (ROWS, ROWS)
    vm = pltpu.VMEM
    scratch = (
        [vm(full, BF16)] * 5
        + [
            vm((4, 4, 2, 128, ROWS), BF16),
            vm(full, BF16),
            vm((2, 4, ROWS, 128), F32),
        ]
        + [vm((14, ROWS, 128), BF16)] * 4
        + [
            vm((8, 4, ROWS, 128), BF16),
            vm(full, F32),
            vm(full, BF16),
            vm((4, 4, 2, 128, ROWS), BF16),
            vm((4, 4, 128, ROWS), BF16),
            vm((4, 4, 128, ROWS), BF16),
            vm((4, 2, 64, ROWS), BF16),
            vm((4, 2, 128, ROWS), BF16),
            vm((4, 128, ROWS), BF16),
            vm((128, ROWS), F32),
            vm((3, 128, ROWS), BF16),
            vm((HEADS, ROWS, ROWS), BF16),
            vm(full, F32),
            vm(full, F32),
        ]
        + [vm(full, BF16)] * 3
        + [
            vm((2, HEADS, DH, DH), F32),
            vm((2, HEADS, DH, DH), BF16),
            vm((2, HEADS, DH, DH), BF16),
            vm((2, 2, DH, DH), BF16),
            vm((2, 3, 2, DH, DH), BF16),
            vm((2, 2, DH, DH), BF16),
            vm((2, 3, 2, DH, DH), BF16),
            vm((2, 2, DH, DH), BF16),
            vm((2, 2, DH, DH), BF16),
            vm((2, 2, DH, DH), F32),
            vm((2, HEADS, DH, DH), BF16),
        ]
    )
    dma = pltpu.SemaphoreType.DMA
    scratch += [
        dma((5,)), dma((5,)), dma((2, 14)), dma((2, 14)), dma((4,)), dma((3,)), dma((16,)), dma((16,)),
        dma((3,)), dma((2, 8)), dma((2, 4)), dma((6,)), dma((16,)), dma((3,)), dma((3,)),
    ]
    anywhere = pl.BlockSpec(memory_space=pl.ANY)

    arguments = (query_rows, key_rows, value_rows, out_weight, target_rows)

    def body(*refs):
        kernel(1.0 / math.sqrt(total_rows), *refs)

    shapes = (rows, rows, rows, rows, jax.ShapeDtypeStruct((128, ROWS), F32))
    results = pl.pallas_call(
        body,
        out_shape=shapes,
        in_specs=[pl.BlockSpec(memory_space=pltpu.HBM)] * 5,
        out_specs=(anywhere,) * 5,
        scratch_shapes=scratch,
        compiler_params=pltpu.CompilerParams(
            collective_id=0, has_side_effects=True, vmem_limit_bytes=48 * 1024 * 1024
        ),
        name="linear_attention",
    )(*(pltpu.with_memory_space_constraint(a, pltpu.HBM) for a in arguments))
    return pl.pallas_call(
        write_out,
        out_shape=shapes,
        in_specs=[anywhere] * 5,
        out_specs=(pl.BlockSpec(memory_space=pltpu.HBM),) * 5,
        scratch_shapes=[dma((5,))],
        compiler_params=pltpu.CompilerParams(vmem_limit_bytes=1024 * 1024),
        name="write_out",
    )(*results)


def solution(mesh):
    torus = Mesh(
        mesh.devices.reshape(4, 4, 2, mesh.shape["head"]), ("seq_0", "seq_1", "seq_2", "head")
    )
    spec = P(SEQ, "head")
    return jax.shard_map(
        on_device, mesh=torus, in_specs=(spec,) * 5, out_specs=(spec,) * 5, check_vma=False
    )
```

```python
import math

import jax
import jax.numpy as jnp
from jax import lax
from jax.experimental import pallas as pl
from jax.experimental.pallas import tpu as pltpu
from jax.sharding import Mesh
from jax.sharding import PartitionSpec as P

DH = 128
ROWS = 512
HEADS = 4
SEQ = ("seq_0", "seq_1", "seq_2")
MESH = pl.DeviceIdType.MESH
F32 = jnp.float32
BF16 = jnp.bfloat16
NT = (((1,), (1,)), ((), ()))
NN = (((1,), (0,)), ((), ()))
TN = (((0,), (0,)), ((), ()))


def dot(a, b, dims):
    return lax.dot_general(a, b, dims, preferred_element_type=F32)


def remote(src, dst, send, recv, **device):
    return pltpu.make_async_remote_copy(
        src_ref=src, dst_ref=dst, send_sem=send, recv_sem=recv, device_id=device, device_id_type=MESH
    )


def wait_bytes(ref, sem):
    pltpu.make_async_copy(ref, ref, sem).wait()


def kernel(
    weight_factor,
    q_in, k_in, v_in, w_in, t_in,
    out_o, gq_o, gk_o, gv_o, gw_o,
    qb, kb, vb, tb, scaled, wf, att, pb, su, sd, ru, rd, res, da, dab, dw, cw, xs, xh, xr, ysend, yown, yrecv,
    scores, gk_acc, gv_acc, oq, ok, ov,
    tot, loc, sib, ct, xrc, rt, yrc, pfs, pfr, px, state, h1, h2, h2r, hk, h3, h3r,
    in_sem, out_sem, rs_recv, ag_recv, z_send, wy_recv, wx_recv, wc_recv, w_send, sc_recv, sc_send,
    dc_recv, dx_recv, dy_recv, d_send, q1_recv, q2_recv, q2_send, q3_recv, q3_send,
):
    y = lax.axis_index("seq_0")
    x = lax.axis_index("seq_1")
    c = lax.axis_index("seq_2")
    z = lax.axis_index("head")
    up = lax.rem(z + 1, 8)
    down = lax.rem(z + 7, 8)
    sibling = 1 - c
    right = lax.rem(x + 1, 4)
    left = lax.rem(x + 3, 4)
    across = lax.rem(x + 2, 4)
    half = lax.div(z, 2)
    turn = 2 * lax.rem(z, 2) - 1
    first_half = pl.ds(0, 64)
    second_half = pl.ds(64, 64)

    def block(k):
        return lax.rem(z + k + 8, 8)

    def level_row(level):
        shift = {1: 0, 2: turn, 3: -turn, 4: 2}[level]
        return lax.rem(half + shift + 4, 4)

    loads = [
        pltpu.make_async_copy(w_in, wf.at[y, x, c], in_sem.at[0]),
        pltpu.make_async_copy(k_in, kb, in_sem.at[1]),
        pltpu.make_async_copy(v_in, vb, in_sem.at[2]),
        pltpu.make_async_copy(q_in, qb, in_sem.at[3]),
        pltpu.make_async_copy(t_in, tb, in_sem.at[4]),
    ]
    for copy in loads:
        copy.start()

    barrier = pltpu.get_barrier_semaphore()
    partners = [{"head": up}, {"head": down}, {"seq_2": sibling}]
    partners += [{"seq_1": lax.rem(x + d, 4)} for d in (1, 2, 3)]
    partners += [{"seq_0": lax.rem(y + d, 4)} for d in (1, 2, 3)]
    for partner in partners:
        pl.semaphore_signal(barrier, inc=1, device_id=partner, device_id_type=MESH)
    pl.semaphore_wait(barrier, len(partners))

    def weight_parts(level):
        return (first_half, second_half) if level >= 3 else (pl.ds(0, 128),)

    def weight_y_copy(level, row, part, d):
        ref = wf.at[row, x, c, weight_parts(level)[part]]
        return remote(ref, ref, w_send.at[0], wy_recv.at[3 * part + d - 1], seq_0=lax.rem(row + d, 4))

    def weight_y(level):
        for d in (2, 3, 1):
            for part in range(len(weight_parts(level))):
                weight_y_copy(level, y, part, d).start()

    def weight_to_core(row, col, slot):
        return remote(
            wf.at[row, col, c], wf.at[row, col, c], w_send.at[2], wc_recv.at[slot], seq_2=sibling
        )

    def weight_side(level, toward_right, part):
        row = level_row(level)
        to, source = (right, left) if toward_right else (left, right)
        side = 0 if toward_right else 1
        if part is None:
            rows = first_half if toward_right else second_half
            sent, got = wf.at[row, source, c, rows], wf.at[row, across, c, rows]
            slot = 4 + side
        else:
            rows = weight_parts(level)[part]
            sent, got = wf.at[row, x, c, rows], wf.at[row, source, c, rows]
            slot = 2 * side + part
        sem = wx_recv.at[6 * (level - 1) + slot]
        return (
            lambda: remote(sent, sent, w_send.at[1], sem, seq_1=to).start(),
            lambda: remote(got, got, w_send.at[1], sem, seq_1=to).wait_recv(),
        )

    def weight_1(level):
        row = level_row(level)
        for part in range(len(weight_parts(level))):

            @pl.when(row != y)
            def _():
                weight_y_copy(level, row, part, lax.rem(y - row + 4, 4)).wait_recv()

            weight_side(level, True, part)[0]()
            weight_side(level, False, part)[0]()
        weight_to_core(row, x, 4 * (level - 1)).start()

    def weight_2(level):
        row = level_row(level)
        last = len(weight_parts(level)) - 1
        weight_side(level, True, 0)[1]()
        weight_side(level, True, None)[0]()
        if last:
            weight_side(level, False, 0)[1]()
        weight_side(level, False, last)[1]()
        weight_side(level, False, None)[0]()
        if last:
            weight_side(level, True, 1)[1]()
        weight_to_core(row, left, 4 * (level - 1) + 1).start()
        weight_to_core(row, right, 4 * (level - 1) + 2).start()

    def weight_3(level):
        row = level_row(level)
        for toward_right in (True, False):
            weight_side(level, toward_right, None)[1]()
        weight_to_core(row, across, 4 * (level - 1) + 3).start()

    def weight_ready(level):
        row = level_row(level)
        for i, col in enumerate((x, left, right, across)):
            slot = 4 * (level - 1) + i
            remote(
                wf.at[row, col, sibling], wf.at[row, col, sibling], w_send.at[2], wc_recv.at[slot],
                seq_2=sibling,
            ).wait_recv()

    loads[0].wait()

    @pl.when(level_row(4) == y)
    def _():
        weight_y(4)

    def head_columns(h):
        return pl.ds(pl.multiple_of(h * DH, DH), DH)

    def scan_begin(n):
        loc[n] = tot[n].astype(BF16)
        remote(loc.at[n], sib.at[n], sc_send.at[n, 0], sc_recv.at[n, 0], seq_2=sibling).start()

    def scan_x_copy(n, i, d):
        return remote(
            ct.at[n, i], xrc.at[n, d - 1, i], sc_send.at[n, 1], sc_recv.at[n, 3 * i + d],
            seq_1=lax.rem(x + d, 4),
        )

    def scan_y_copy(n, i, d):
        return remote(
            rt.at[n, i], yrc.at[n, d - 1, i], sc_send.at[n, 2], sc_recv.at[n, 6 + 3 * i + d],
            seq_0=lax.rem(y + d, 4),
        )

    def scan_core_copy(n, i):
        return remote(
            pfs.at[n, i], pfr.at[n, i], sc_send.at[n, 3], sc_recv.at[n, 13 + i], seq_2=sibling
        )

    def scan_x(n):
        remote(sib.at[n], sib.at[n], sc_send.at[n, 0], sc_recv.at[n, 0], seq_2=sibling).wait_recv()
        for i in (0, 1):
            chip = tot[n, 2 * c + i] + sib[n, 2 * c + i].astype(F32)
            ct[n, i] = chip.astype(BF16)
            for d in (2, 1, 3):
                scan_x_copy(n, i, d).start()

    def scan_y(n, reverse):
        for i in (0, 1):
            total = ct[n, i].astype(F32)
            passed = jnp.zeros((DH, DH), F32)
            for d in (1, 3, 2):
                scan_x_copy(n, i, d).wait_recv()
                piece = xrc[n, d - 1, i].astype(F32)
                total = total + piece
                counts = (d > x) if reverse else (d <= x)
                passed = passed + piece * counts.astype(F32)
            rt[n, i] = total.astype(BF16)
            px[n, i] = passed
            for d in (2, 1, 3):
                scan_y_copy(n, i, d).start()

    def scan_core(n, reverse):
        for i in (0, 1):
            passed = px[n, i]
            for d in (1, 3, 2):
                scan_y_copy(n, i, d).wait_recv()
                counts = (d > y) if reverse else (d <= y)
                passed = passed + yrc[n, d - 1, i].astype(F32) * counts.astype(F32)
            px[n, i] = passed
            pfs[n, i] = passed.astype(BF16)
            scan_core_copy(n, i).start()

    def scan_end(n, reverse):
        own_core = (c == 0) if reverse else (c == 1)
        factor = own_core.astype(F32)
        for i in (0, 1):
            ours, theirs = 2 * c + i, 2 * sibling + i
            state[n, ours] = (px[n, i] + sib[n, ours].astype(F32) * factor).astype(BF16)
            scan_core_copy(n, i).wait_recv()
            state[n, theirs] = (pfr[n, i].astype(F32) + sib[n, theirs].astype(F32) * factor).astype(BF16)

    loads[1].wait()
    loads[2].wait()

    @pl.loop(0, HEADS)
    def _(h):
        cols = head_columns(h)
        tot[0, h] = dot(kb[:, cols], vb[:, cols], TN)

    scan_begin(0)

    @pl.when(level_row(3) == y)
    def _():
        weight_y(3)

    first = lax.rem((y * 4 + x) * 2 + c, 32) * ROWS
    positions = (first + lax.broadcasted_iota(jnp.int32, (ROWS, 1), 0) + 1).astype(F32)
    scale = lax.rsqrt(F32(DH) * positions)
    loads[3].wait()
    scaled[...] = (qb[...].astype(F32) * scale).astype(BF16)
    scan_x(0)

    causal = lax.broadcasted_iota(jnp.int32, (ROWS, ROWS), 0) >= lax.broadcasted_iota(
        jnp.int32, (ROWS, ROWS), 1
    )

    @pl.loop(0, HEADS)
    def _(h):
        cols = head_columns(h)
        s = dot(scaled[:, cols], kb[:, cols], NT)
        scores[h] = jnp.where(causal, s, 0.0).astype(BF16)

    weight_1(4)

    @pl.loop(0, HEADS)
    def _(h):
        cols = head_columns(h)
        gk_acc[:, cols] = dot(scores[h], vb[:, cols], NN)

    scan_y(0, False)

    @pl.when(jnp.logical_and(level_row(4) != y, level_row(3) != y))
    def _():
        weight_y(1)

    weight_1(3)
    weight_2(4)
    scan_core(0, False)
    weight_3(4)
    scan_end(0, False)

    @pl.loop(0, HEADS)
    def _(h):
        cols = head_columns(h)
        att[:, cols] = (dot(scaled[:, cols], state[0, h], NN) + gk_acc[:, cols]).astype(BF16)

    up_order = (2 + c, 3 - c, c, 1 - c)
    down_order = (c, 1 - c, 2 + c, 3 - c)
    gather_order = (c, 1 - c, 2 + c, 3 - c)

    def block_cols(b):
        return lax.div(b, 2), pl.ds(2 * lax.rem(b, 2), 2)

    def weight_block(b):
        row, cols = block_cols(b)
        return wf[row, cols].reshape(ROWS, ROWS)

    def partial(u, b):
        value = dot(att[...], weight_block(b), NT)
        for r in range(4):
            pb[u, r] = value[:, r * 128 : (r + 1) * 128]

    def reduce_copy(u, idx):
        src, dst = (su, ru) if u == 0 else (sd, rd)
        return remote(
            src.at[idx], dst.at[idx], z_send.at[u], rs_recv.at[u, idx], head=up if u == 0 else down
        )

    def reduce_send(u, idx, r, received):
        src, dst = (su, ru) if u == 0 else (sd, rd)
        value = pb[u, r]
        if received is not None:
            reduce_copy(u, received).wait_recv()
            value = value + dst[received].astype(F32)
        src[idx] = value.astype(BF16)
        reduce_copy(u, idx).start()

    row4, cols4 = block_cols(block(4))
    for i, core in enumerate((c, sibling)):
        if i == 1:
            weight_ready(4)
        value = dot(att[...], wf[row4, cols4, core].reshape(256, ROWS), NT)
        su[i] = value[:, 0:128].astype(BF16)
        sd[i] = value[:, 128:256].astype(BF16)
        reduce_copy(0, i).start()
        reduce_copy(1, i).start()
    weight_2(3)
    weight_1(2)
    weight_3(3)
    weight_ready(3)
    partial(0, block(3))
    partial(1, block(-3))
    for j in range(4):
        reduce_send(0, 2 + j, up_order[j], None if j < 2 else j - 2)
        reduce_send(1, 2 + j, down_order[j], None if j < 2 else j - 2)
    for k in (2, 1):
        weight_2(k)
        if k == 2:
            weight_1(1)
        weight_3(k)
        weight_ready(k)
        partial(0, block(k))
        partial(1, block(-k))
        for j in range(4):
            idx = 4 * (3 - k) + 2 + j
            reduce_send(0, idx, up_order[j], idx - 4)
            reduce_send(1, idx, down_order[j], idx - 4)
    partial(0, z)

    def gather_copy(u, idx, b, r):
        return remote(
            res.at[b, r], res.at[b, r], z_send.at[2 + u], ag_recv.at[u, idx], head=up if u == 0 else down
        )

    loads[4].wait()
    for j, r in enumerate(gather_order):
        i_up = 10 + (2, 3, 0, 1)[j]
        i_down = 10 + j
        reduce_copy(0, i_up).wait_recv()
        reduce_copy(1, i_down).wait_recv()
        value = (pb[0, r] + ru[i_up].astype(F32) + rd[i_down].astype(F32)).astype(BF16)
        cols = pl.ds(pl.multiple_of(r * 128, 128), 128)
        ov[:, cols] = value
        res[z, r] = (value.astype(F32) - tb[:, cols].astype(F32)).astype(BF16)
        gather_copy(0, j, z, r).start()
        gather_copy(1, j, z, r).start()
    out_copy = pltpu.make_async_copy(ov, out_o, out_sem.at[0])
    out_copy.start()

    def residual_block(b, pieces):
        return jnp.concatenate([res[b, r] for r in pieces], axis=1)

    def grads(b, begin=False):
        term = dot(residual_block(b, range(4)), weight_block(b), NN)
        da[...] = term if begin else da[...] + term

    def weight_grads(b):
        row, cols = block_cols(b)
        d_b = dot(residual_block(b, range(4)), att[...], TN).astype(BF16)
        dw[row, cols] = d_b.reshape(2, 2, 128, ROWS)

    def dw_to_core(row, cols, level, slot):
        return remote(
            dw.at[row, cols, sibling], cw.at[level - 1, cols], d_send.at[0], dc_recv.at[slot], seq_2=sibling
        )

    every = pl.ds(0, 4)

    def dw_side(level, toward_right, whole):
        to = right if toward_right else left
        side = 0 if toward_right else 1
        sem = dx_recv.at[4 * (level - 1) + side + (0 if whole else 2)]
        if whole:
            return remote(xs.at[level - 1, to], xr.at[level - 1, side], d_send.at[1], sem, seq_1=to)
        part = first_half if toward_right else second_half
        return remote(
            xs.at[level - 1, across, part], xh.at[level - 1, side], d_send.at[1], sem, seq_1=to
        )

    def dw_1(level):
        row = level_row(level)
        dw_to_core(row, every, level, level - 1).wait_recv()
        for i, to in enumerate((across, right, left, x)):
            xs[level - 1, to] = (
                dw[row, to, c].astype(F32) + cw[level - 1, to].astype(F32)
            ).astype(BF16)
            if i == 0:
                dw_side(level, True, False).start()
                dw_side(level, False, False).start()

    def dw_2(level):
        for side, toward_right in enumerate((True, False)):
            to = right if toward_right else left
            part = first_half if toward_right else second_half
            dw_side(level, toward_right, False).wait_recv()
            value = xs[level - 1, to, part].astype(F32) + xh[level - 1, side].astype(F32)
            xs[level - 1, to, part] = value.astype(BF16)
            dw_side(level, toward_right, True).start()

    def dw_3(level):
        row = level_row(level)
        total = xs[level - 1, x].astype(F32)
        for side, toward_right in enumerate((True, False)):
            dw_side(level, toward_right, True).wait_recv()
            total = total + xr[level - 1, side].astype(F32)

        @pl.when(row == y)
        def _():
            yown[...] = total

        @pl.when(row != y)
        def _():
            ysend[level - 1] = total.astype(BF16)
            d = lax.rem(row - y + 4, 4)
            remote(
                ysend.at[level - 1], yrecv.at[d - 1], d_send.at[2], dy_recv.at[d - 1], seq_0=row
            ).start()

    first_col = 2 * lax.rem(block(4), 2)
    other_col = 2 - first_col
    row3 = level_row(3)
    piece_cols = (
        first_col, first_col + 1, other_col, other_col, other_col + 1, other_col + 1, first_col, first_col + 1
    )
    piece_rows = (row3, row3, row3, row4, row3, row4, row4, row4)
    piece_group = (2, 2, 2, 3, 2, 3, 3, 3)

    def lanes(q):
        return pl.ds(pl.multiple_of(q * 128, 128), 128)

    def along(x_axis, to):
        return {"seq_1": to} if x_axis else {"seq_0": to}

    def piece_to_core(p, count=1):
        cols = pl.ds(piece_cols[p], count)
        return remote(
            dw.at[piece_rows[p], cols, sibling], cw.at[piece_group[p], cols], d_send.at[0],
            dc_recv.at[2 + p], seq_2=sibling,
        )

    def quarter_copy(p, d):
        x_axis = p < 6
        to = lax.rem((x if x_axis else y) + d, 4)
        return remote(
            xs.at[piece_group[p], piece_cols[p], :, lanes(to)], h1.at[p, d - 1], d_send.at[3],
            q1_recv.at[p, d - 1], **along(x_axis, to),
        )

    def quarter_place(p):
        to_col = lax.rem(piece_cols[p] - x + 4, 4)
        to_row = lax.rem(piece_rows[p] - y + 4, 4)
        return (to_row, to_col) if p < 6 else (to_col, to_row)

    def quarter_1(p):
        row, col, group = piece_rows[p], piece_cols[p], piece_group[p]
        if p == 0:
            piece_to_core(0, 2).wait_recv()
        elif p != 1:
            piece_to_core(p).wait_recv()
        xs[group, col] = (dw[row, col, c].astype(F32) + cw[group, col].astype(F32)).astype(BF16)
        for d in (2, 1, 3):
            quarter_copy(p, d).start()

    def quarter_2(p):
        total = xs[piece_group[p], piece_cols[p], :, lanes(x if p < 6 else y)].astype(F32)
        for d in (1, 3, 2):
            quarter_copy(p, d).wait_recv()
            total = total + h1[p, d - 1].astype(F32)
        away, _ = quarter_place(p)
        hk[p] = total

        @pl.when(away != 0)
        def _():
            h2[p] = total.astype(BF16)
            to = piece_rows[p] if p < 6 else piece_cols[p]
            remote(
                h2.at[p], h2r.at[p, away - 1], q2_send.at[p], q2_recv.at[p, away - 1], **along(p >= 6, to)
            ).start()

    def quarter_3(p):
        away, rest = quarter_place(p)

        @pl.when(away == 0)
        def _():
            total = hk[p]
            for d in (1, 3, 2):
                remote(
                    h2r.at[p, d - 1], h2r.at[p, d - 1], q2_send.at[p], q2_recv.at[p, d - 1],
                    **along(p >= 6, lax.rem((x if p >= 6 else y) + d, 4)),
                ).wait_recv()
                total = total + h2r[p, d - 1].astype(F32)

            @pl.when(rest == 0)
            def _():
                yown[:, lanes(x if p < 6 else y)] = total

            @pl.when(rest != 0)
            def _():
                h3[p] = total.astype(BF16)
                group = 0 if p < 6 else 1
                to = piece_cols[p] if p < 6 else piece_rows[p]
                remote(
                    h3.at[p], h3r.at[group, rest - 1], q3_send.at[p], q3_recv.at[group, rest - 1],
                    **along(p < 6, to),
                ).start()

    def quarter_end(group):
        axis_place = x if group == 0 else y
        for d in (1, 3, 2):
            remote(
                h3r.at[group, d - 1], h3r.at[group, d - 1], q3_send.at[0], q3_recv.at[group, d - 1],
                **along(group == 0, lax.rem(axis_place + d, 4)),
            ).wait_recv()
            yown[:, lanes(lax.rem(axis_place - d + 4, 4))] = h3r[group, d - 1].astype(F32)

    grads(z, begin=True)
    weight_grads(z)
    def half_block(b, i):
        row, cols = block_cols(b)
        col = 2 * lax.rem(b, 2) + i
        pieces = residual_block(b, (2 * i, 2 * i + 1))
        d_b = dot(pieces, att[...], TN).astype(BF16)
        dw[row, col] = d_b.reshape(2, 128, ROWS)
        return dot(pieces, wf[row, col].reshape(256, ROWS), NN)

    def both_halves(i):
        @pl.loop(0, 2)
        def _(u):
            da[...] += half_block(block(3 * (2 * u - 1)), i)

    def chunk(k, j):
        r = gather_order[j]
        for u in (0, 1):
            b = block(-k if u == 0 else k)
            gather_copy(u, 4 * (k - 1) + j, b, r).wait_recv()
            if k < 3:
                gather_copy(u, 4 * k + j, b, r).start()
            elif j % 2 == u:
                gather_copy(u, 12 + j // 2, b, r).start()

    for k in (1, 2):
        for j in range(4):
            chunk(k, j)
            if k == 2 and j == 0:
                dw_1(1)
            if k == 2 and j == 2:
                dw_2(1)

        @pl.loop(0, 2)
        def _(u, k=k):
            b = block(k * (2 * u - 1))
            grads(b)
            weight_grads(b)

        dw_to_core(level_row(k), every, k, k - 1).start()
    piece_to_core(0, 2).start()
    chunk(3, 0)
    dw_1(2)
    quarter_1(0)
    quarter_1(1)
    chunk(3, 1)
    both_halves(0)
    piece_to_core(2).start()
    piece_to_core(3).start()
    dw_3(1)
    chunk(3, 2)
    dw_2(2)
    quarter_1(2)
    quarter_1(3)
    quarter_2(0)
    quarter_2(1)
    chunk(3, 3)
    both_halves(1)
    piece_to_core(4).start()
    piece_to_core(5).start()
    dw_3(2)

    b4 = block(4)

    def last_half(i):
        gather_copy(0, 12 + i, b4, gather_order[2 * i]).wait_recv()
        gather_copy(1, 12 + i, b4, gather_order[2 * i + 1]).wait_recv()
        term = dot(residual_block(b4, (2 * i, 2 * i + 1)), wf[row4, first_col + i].reshape(256, ROWS), NN)
        if i == 0:
            da[...] += term
        else:
            dab[...] = (da[...] + term).astype(BF16)

    def last_weight_half(i):
        d_b = dot(residual_block(b4, (2 * i, 2 * i + 1)), att[...], TN).astype(BF16)
        dw[row4, first_col + i] = d_b.reshape(2, 128, ROWS)
        piece_to_core(6 + i).start()

    last_half(0)
    last_weight_half(0)
    quarter_2(2)
    quarter_2(3)
    quarter_1(4)
    quarter_1(5)
    last_half(1)

    @pl.loop(0, HEADS)
    def _(h):
        cols = head_columns(h)
        tot[1, h] = dot(scaled[:, cols], dab[:, cols], TN)

    scan_begin(1)
    last_weight_half(1)
    scan_x(1)
    quarter_1(6)
    quarter_1(7)
    quarter_3(0)
    quarter_3(1)

    def gradient_pair(start):
        @pl.loop(start, start + 2)
        def _(h):
            cols = head_columns(h)
            mixed = jnp.where(causal, dot(dab[:, cols], vb[:, cols], NT), 0.0).astype(BF16)
            g = dot(dab[:, cols], state[0, h], NT) + dot(mixed, kb[:, cols], NN)
            oq[:, cols] = (g * scale).astype(BF16)
            gk_acc[:, cols] = dot(mixed, scaled[:, cols], TN)
            gv_acc[:, cols] = dot(scores[h], dab[:, cols], TN)

    gradient_pair(0)
    quarter_2(4)
    quarter_2(5)
    quarter_3(2)
    quarter_3(3)
    gradient_pair(2)
    scan_y(1, True)
    q_copy = pltpu.make_async_copy(oq, gq_o, out_sem.at[1])
    q_copy.start()
    quarter_2(6)
    quarter_2(7)
    for p in range(4, 8):
        quarter_3(p)
    scan_core(1, True)
    scan_end(1, True)
    out_copy.wait()

    @pl.loop(0, HEADS)
    def _(h):
        cols = head_columns(h)
        ok[:, cols] = (gk_acc[:, cols] + dot(vb[:, cols], state[1, h], NT)).astype(BF16)
        ov[:, cols] = (gv_acc[:, cols] + dot(kb[:, cols], state[1, h], NN)).astype(BF16)

    k_copy = pltpu.make_async_copy(ok, gk_o, out_sem.at[2])
    k_copy.start()
    v_copy = pltpu.make_async_copy(ov, gv_o, out_sem.at[3])
    v_copy.start()

    in_last = jnp.logical_or(row3 == y, row4 == y)

    @pl.when(jnp.logical_not(in_last))
    def _():
        total = yown[...]
        for d in (1, 3, 2):
            remote(
                yrecv.at[d - 1], yrecv.at[d - 1], d_send.at[2], dy_recv.at[d - 1], seq_0=lax.rem(y + d, 4)
            ).wait_recv()
            total = total + yrecv[d - 1].astype(F32)
        yown[...] = total

    in_second = jnp.logical_and(row4 == y, lax.div(x, 2) == lax.div(first_col, 2))

    @pl.when(jnp.logical_and(in_last, jnp.logical_not(in_second)))
    def _():
        quarter_end(0)

    @pl.when(in_second)
    def _():
        quarter_end(1)

    yown[...] = yown[...] * weight_factor
    w_copy = pltpu.make_async_copy(yown, gw_o, out_sem.at[4])
    w_copy.start()

    wait_bytes(su, z_send.at[0])
    wait_bytes(sd, z_send.at[1])
    wait_bytes(su, z_send.at[2])
    wait_bytes(sd, z_send.at[3])
    wait_bytes(yrecv, w_send.at[0])
    wait_bytes(su.at[pl.ds(0, 12)], w_send.at[1])
    wait_bytes(xs, w_send.at[2])
    wait_bytes(cw, d_send.at[0])
    wait_bytes(su.at[pl.ds(0, 6)], d_send.at[1])

    @pl.when(in_last)
    def _():
        wait_bytes(yrecv.at[pl.ds(0, 2)], d_send.at[2])

    @pl.when(jnp.logical_not(in_last))
    def _():
        wait_bytes(yrecv.at[0], d_send.at[2])

    wait_bytes(su.at[pl.ds(0, 6)], d_send.at[3])
    for p in range(8):
        away, rest = quarter_place(p)

        @pl.when(away != 0)
        def _(p=p):
            wait_bytes(h2.at[p], q2_send.at[p])

        @pl.when(jnp.logical_and(away == 0, rest != 0))
        def _(p=p):
            wait_bytes(h3.at[p], q3_send.at[p])

    for n in (0, 1):
        wait_bytes(loc.at[n], sc_send.at[n, 0])
        wait_bytes(xrc.at[n], sc_send.at[n, 1])
        wait_bytes(yrc.at[n], sc_send.at[n, 2])
        wait_bytes(pfs.at[n], sc_send.at[n, 3])
    for copy in (q_copy, k_copy, v_copy, w_copy):
        copy.wait()


def write_out(*refs):
    sems = refs[-1]
    copies = [pltpu.make_async_copy(refs[i], refs[5 + i], sems.at[i]) for i in range(5)]
    for copy in copies:
        copy.start()
    for copy in copies:
        copy.wait()


def on_device(query_rows, key_rows, value_rows, out_weight, target_rows):
    rows = jax.ShapeDtypeStruct((ROWS, ROWS), BF16)
    total_rows = query_rows.shape[0] * lax.axis_size(SEQ)
    full = (ROWS, ROWS)
    vm = pltpu.VMEM
    scratch = (
        [vm(full, BF16)] * 5
        + [
            vm((4, 4, 2, 128, ROWS), BF16),
            vm(full, BF16),
            vm((2, 4, ROWS, 128), F32),
        ]
        + [vm((14, ROWS, 128), BF16)] * 4
        + [
            vm((8, 4, ROWS, 128), BF16),
            vm(full, F32),
            vm(full, BF16),
            vm((4, 4, 2, 128, ROWS), BF16),
            vm((4, 4, 128, ROWS), BF16),
            vm((4, 4, 128, ROWS), BF16),
            vm((4, 2, 64, ROWS), BF16),
            vm((4, 2, 128, ROWS), BF16),
            vm((4, 128, ROWS), BF16),
            vm((128, ROWS), F32),
            vm((3, 128, ROWS), BF16),
            vm((HEADS, ROWS, ROWS), BF16),
            vm(full, F32),
            vm(full, F32),
        ]
        + [vm(full, BF16)] * 3
        + [
            vm((2, HEADS, DH, DH), F32),
            vm((2, HEADS, DH, DH), BF16),
            vm((2, HEADS, DH, DH), BF16),
            vm((2, 2, DH, DH), BF16),
            vm((2, 3, 2, DH, DH), BF16),
            vm((2, 2, DH, DH), BF16),
            vm((2, 3, 2, DH, DH), BF16),
            vm((2, 2, DH, DH), BF16),
            vm((2, 2, DH, DH), BF16),
            vm((2, 2, DH, DH), F32),
            vm((2, HEADS, DH, DH), BF16),
            vm((8, 3, 128, 128), BF16),
            vm((8, 128, 128), BF16),
            vm((8, 3, 128, 128), BF16),
            vm((8, 128, 128), F32),
            vm((8, 128, 128), BF16),
            vm((2, 3, 128, 128), BF16),
        ]
    )
    dma = pltpu.SemaphoreType.DMA
    scratch += [
        dma((5,)), dma((5,)), dma((2, 14)), dma((2, 14)), dma((4,)), dma((6,)), dma((24,)), dma((16,)),
        dma((3,)), dma((2, 15)), dma((2, 4)), dma((10,)), dma((8,)), dma((3,)), dma((4,)),
        dma((8, 3)), dma((8, 3)), dma((8,)), dma((2, 3)), dma((8,)),
    ]
    anywhere = pl.BlockSpec(memory_space=pl.ANY)

    arguments = (query_rows, key_rows, value_rows, out_weight, target_rows)

    def body(*refs):
        kernel(1.0 / math.sqrt(total_rows), *refs)

    shapes = (rows, rows, rows, rows, jax.ShapeDtypeStruct((128, ROWS), F32))
    results = pl.pallas_call(
        body,
        out_shape=shapes,
        in_specs=[pl.BlockSpec(memory_space=pltpu.HBM)] * 5,
        out_specs=(anywhere,) * 5,
        scratch_shapes=scratch,
        compiler_params=pltpu.CompilerParams(
            collective_id=0, has_side_effects=True, vmem_limit_bytes=48 * 1024 * 1024
        ),
        name="linear_attention",
    )(*(pltpu.with_memory_space_constraint(a, pltpu.HBM) for a in arguments))
    return pl.pallas_call(
        write_out,
        out_shape=shapes,
        in_specs=[anywhere] * 5,
        out_specs=(pl.BlockSpec(memory_space=pltpu.HBM),) * 5,
        scratch_shapes=[dma((5,))],
        compiler_params=pltpu.CompilerParams(vmem_limit_bytes=1024 * 1024),
        name="write_out",
    )(*results)


def solution(mesh):
    torus = Mesh(
        mesh.devices.reshape(4, 4, 2, mesh.shape["head"]), ("seq_0", "seq_1", "seq_2", "head")
    )
    spec = P(SEQ, "head")
    return jax.shard_map(
        on_device, mesh=torus, in_specs=(spec,) * 5, out_specs=(spec,) * 5, check_vma=False
    )
```

```python
import math

import jax
import jax.numpy as jnp
from jax import lax
from jax.experimental import pallas as pl
from jax.experimental.pallas import tpu as pltpu
from jax.sharding import Mesh
from jax.sharding import PartitionSpec as P

DH = 128
ROWS = 512
HEADS = 4
SEQ = ("seq_0", "seq_1", "seq_2")
MESH = pl.DeviceIdType.MESH
F32 = jnp.float32
BF16 = jnp.bfloat16
NT = (((1,), (1,)), ((), ()))
NN = (((1,), (0,)), ((), ()))
TN = (((0,), (0,)), ((), ()))


def dot(a, b, dims):
    return lax.dot_general(a, b, dims, preferred_element_type=F32)


def remote(src, dst, send, recv, **device):
    return pltpu.make_async_remote_copy(
        src_ref=src, dst_ref=dst, send_sem=send, recv_sem=recv, device_id=device, device_id_type=MESH
    )


def wait_bytes(ref, sem):
    pltpu.make_async_copy(ref, ref, sem).wait()


def kernel(
    weight_factor,
    q_in, k_in, v_in, w_in, t_in,
    out_o, gq_o, gk_o, gv_o, gw_o,
    qb, kb, vb, tb, scaled, wf, att, pb, su, sd, ru, rd, res, da, dab, dw, cw, xs, xh, xr, ysend, yown, yrecv,
    scores, gk_acc, gv_acc, oq, ok, ov,
    tot, loc, sib, ct, xrc, rt, yrc, pfs, pfr, px, state, h1, h2, h2r, hk, h3, h3r,
    in_sem, out_sem, rs_recv, ag_recv, z_send, wy_recv, wx_recv, wc_recv, w_send, sc_recv, sc_send,
    dc_recv, dx_recv, dy_recv, d_send, q1_recv, q2_recv, q2_send, q3_recv, q3_send,
):
    y = lax.axis_index("seq_0")
    x = lax.axis_index("seq_1")
    c = lax.axis_index("seq_2")
    z = lax.axis_index("head")
    up = lax.rem(z + 1, 8)
    down = lax.rem(z + 7, 8)
    sibling = 1 - c
    right = lax.rem(x + 1, 4)
    left = lax.rem(x + 3, 4)
    across = lax.rem(x + 2, 4)
    half = lax.div(z, 2)
    turn = 2 * lax.rem(z, 2) - 1
    first_half = pl.ds(0, 64)
    second_half = pl.ds(64, 64)

    def block(k):
        return lax.rem(z + k + 8, 8)

    def level_row(level):
        shift = {1: 0, 2: turn, 3: -turn, 4: 2}[level]
        return lax.rem(half + shift + 4, 4)

    loads = [
        pltpu.make_async_copy(w_in, wf.at[y, x, c], in_sem.at[0]),
        pltpu.make_async_copy(k_in, kb, in_sem.at[1]),
        pltpu.make_async_copy(v_in, vb, in_sem.at[2]),
        pltpu.make_async_copy(q_in, qb, in_sem.at[3]),
        pltpu.make_async_copy(t_in, tb, in_sem.at[4]),
    ]
    for copy in loads:
        copy.start()

    barrier = pltpu.get_barrier_semaphore()
    partners = [{"head": up}, {"head": down}, {"seq_2": sibling}]
    partners += [{"seq_1": lax.rem(x + d, 4)} for d in (1, 2, 3)]
    partners += [{"seq_0": lax.rem(y + d, 4)} for d in (1, 2, 3)]
    for partner in partners:
        pl.semaphore_signal(barrier, inc=1, device_id=partner, device_id_type=MESH)
    pl.semaphore_wait(barrier, len(partners))

    def weight_parts(level):
        return (first_half, second_half) if level >= 3 else (pl.ds(0, 128),)

    def weight_y_copy(level, row, part, d):
        ref = wf.at[row, x, c, weight_parts(level)[part]]
        return remote(ref, ref, w_send.at[0], wy_recv.at[3 * part + d - 1], seq_0=lax.rem(row + d, 4))

    def weight_y(level):
        for d in (2, 3, 1):
            for part in range(len(weight_parts(level))):
                weight_y_copy(level, y, part, d).start()

    def weight_to_core(row, col, slot):
        return remote(
            wf.at[row, col, c], wf.at[row, col, c], w_send.at[2], wc_recv.at[slot], seq_2=sibling
        )

    def weight_side(level, toward_right, part):
        row = level_row(level)
        to, source = (right, left) if toward_right else (left, right)
        side = 0 if toward_right else 1
        if part is None:
            rows = first_half if toward_right else second_half
            sent, got = wf.at[row, source, c, rows], wf.at[row, across, c, rows]
            slot = 4 + side
        else:
            rows = weight_parts(level)[part]
            sent, got = wf.at[row, x, c, rows], wf.at[row, source, c, rows]
            slot = 2 * side + part
        sem = wx_recv.at[6 * (level - 1) + slot]
        return (
            lambda: remote(sent, sent, w_send.at[1], sem, seq_1=to).start(),
            lambda: remote(got, got, w_send.at[1], sem, seq_1=to).wait_recv(),
        )

    def weight_1(level):
        row = level_row(level)
        for part in range(len(weight_parts(level))):

            @pl.when(row != y)
            def _():
                weight_y_copy(level, row, part, lax.rem(y - row + 4, 4)).wait_recv()

            weight_side(level, True, part)[0]()
            weight_side(level, False, part)[0]()
        weight_to_core(row, x, 4 * (level - 1)).start()

    def weight_2(level):
        row = level_row(level)
        last = len(weight_parts(level)) - 1
        weight_side(level, True, 0)[1]()
        weight_side(level, True, None)[0]()
        if last:
            weight_side(level, False, 0)[1]()
        weight_side(level, False, last)[1]()
        weight_side(level, False, None)[0]()
        if last:
            weight_side(level, True, 1)[1]()
        weight_to_core(row, left, 4 * (level - 1) + 1).start()
        weight_to_core(row, right, 4 * (level - 1) + 2).start()

    def weight_3(level):
        row = level_row(level)
        for toward_right in (True, False):
            weight_side(level, toward_right, None)[1]()
        weight_to_core(row, across, 4 * (level - 1) + 3).start()

    def weight_ready(level):
        row = level_row(level)
        for i, col in enumerate((x, left, right, across)):
            slot = 4 * (level - 1) + i
            remote(
                wf.at[row, col, sibling], wf.at[row, col, sibling], w_send.at[2], wc_recv.at[slot],
                seq_2=sibling,
            ).wait_recv()

    loads[0].wait()

    @pl.when(level_row(4) == y)
    def _():
        weight_y(4)

    def head_columns(h):
        return pl.ds(h * DH, DH)

    def scan_begin(n):
        loc[n] = tot[n].astype(BF16)
        remote(loc.at[n], sib.at[n], sc_send.at[n, 0], sc_recv.at[n, 0], seq_2=sibling).start()

    def scan_x_copy(n, i, d):
        return remote(
            ct.at[n, i], xrc.at[n, d - 1, i], sc_send.at[n, 1], sc_recv.at[n, 3 * i + d],
            seq_1=lax.rem(x + d, 4),
        )

    def scan_y_copy(n, i, d):
        return remote(
            rt.at[n, i], yrc.at[n, d - 1, i], sc_send.at[n, 2], sc_recv.at[n, 6 + 3 * i + d],
            seq_0=lax.rem(y + d, 4),
        )

    def scan_core_copy(n, i):
        return remote(
            pfs.at[n, i], pfr.at[n, i], sc_send.at[n, 3], sc_recv.at[n, 13 + i], seq_2=sibling
        )

    def scan_x(n):
        remote(sib.at[n], sib.at[n], sc_send.at[n, 0], sc_recv.at[n, 0], seq_2=sibling).wait_recv()
        for i in (0, 1):
            chip = tot[n, 2 * c + i] + sib[n, 2 * c + i].astype(F32)
            ct[n, i] = chip.astype(BF16)
            for d in (2, 1, 3):
                scan_x_copy(n, i, d).start()

    def scan_y(n, reverse):
        for i in (0, 1):
            total = ct[n, i].astype(F32)
            passed = jnp.zeros((DH, DH), F32)
            for d in (1, 3, 2):
                scan_x_copy(n, i, d).wait_recv()
                piece = xrc[n, d - 1, i].astype(F32)
                total = total + piece
                counts = (d > x) if reverse else (d <= x)
                passed = passed + piece * counts.astype(F32)
            rt[n, i] = total.astype(BF16)
            px[n, i] = passed
            for d in (2, 1, 3):
                scan_y_copy(n, i, d).start()

    def scan_core(n, reverse):
        for i in (0, 1):
            passed = px[n, i]
            for d in (1, 3, 2):
                scan_y_copy(n, i, d).wait_recv()
                counts = (d > y) if reverse else (d <= y)
                passed = passed + yrc[n, d - 1, i].astype(F32) * counts.astype(F32)
            px[n, i] = passed
            pfs[n, i] = passed.astype(BF16)
            scan_core_copy(n, i).start()

    def scan_end(n, reverse):
        own_core = (c == 0) if reverse else (c == 1)
        factor = own_core.astype(F32)
        for i in (0, 1):
            ours, theirs = 2 * c + i, 2 * sibling + i
            state[n, ours] = (px[n, i] + sib[n, ours].astype(F32) * factor).astype(BF16)
            scan_core_copy(n, i).wait_recv()
            state[n, theirs] = (pfr[n, i].astype(F32) + sib[n, theirs].astype(F32) * factor).astype(BF16)

    loads[1].wait()
    loads[2].wait()

    for h in range(HEADS):
        cols = head_columns(h)
        tot[0, h] = dot(kb[:, cols], vb[:, cols], TN)

    scan_begin(0)

    @pl.when(level_row(3) == y)
    def _():
        weight_y(3)

    first = lax.rem((y * 4 + x) * 2 + c, 32) * ROWS
    positions = (first + lax.broadcasted_iota(jnp.int32, (ROWS, 1), 0) + 1).astype(F32)
    scale = lax.rsqrt(F32(DH) * positions)
    loads[3].wait()
    scaled[...] = (qb[...].astype(F32) * scale).astype(BF16)
    scan_x(0)

    causal = lax.broadcasted_iota(jnp.int32, (ROWS, ROWS), 0) >= lax.broadcasted_iota(
        jnp.int32, (ROWS, ROWS), 1
    )

    for h in range(HEADS):
        cols = head_columns(h)
        s = dot(scaled[:, cols], kb[:, cols], NT)
        scores[h] = jnp.where(causal, s, 0.0).astype(BF16)

    weight_1(4)

    for h in range(HEADS):
        cols = head_columns(h)
        gk_acc[:, cols] = dot(scores[h], vb[:, cols], NN)

    scan_y(0, False)

    @pl.when(jnp.logical_and(level_row(4) != y, level_row(3) != y))
    def _():
        weight_y(1)

    weight_1(3)
    weight_2(4)
    scan_core(0, False)
    weight_3(4)
    scan_end(0, False)

    for h in range(HEADS):
        cols = head_columns(h)
        att[:, cols] = (dot(scaled[:, cols], state[0, h], NN) + gk_acc[:, cols]).astype(BF16)

    up_order = (2 + c, 3 - c, c, 1 - c)
    down_order = (c, 1 - c, 2 + c, 3 - c)
    gather_order = (c, 1 - c, 2 + c, 3 - c)

    def block_cols(b):
        return lax.div(b, 2), pl.ds(2 * lax.rem(b, 2), 2)

    def weight_block(b):
        row, cols = block_cols(b)
        return wf[row, cols].reshape(ROWS, ROWS)

    def partial(u, b):
        value = dot(att[...], weight_block(b), NT)
        for r in range(4):
            pb[u, r] = value[:, r * 128 : (r + 1) * 128]

    def reduce_copy(u, idx):
        src, dst = (su, ru) if u == 0 else (sd, rd)
        return remote(
            src.at[idx], dst.at[idx], z_send.at[u], rs_recv.at[u, idx], head=up if u == 0 else down
        )

    def reduce_send(u, idx, r, received):
        src, dst = (su, ru) if u == 0 else (sd, rd)
        value = pb[u, r]
        if received is not None:
            reduce_copy(u, received).wait_recv()
            value = value + dst[received].astype(F32)
        src[idx] = value.astype(BF16)
        reduce_copy(u, idx).start()

    row4, cols4 = block_cols(block(4))
    for i, core in enumerate((c, sibling)):
        if i == 1:
            weight_ready(4)
        value = dot(att[...], wf[row4, cols4, core].reshape(256, ROWS), NT)
        su[i] = value[:, 0:128].astype(BF16)
        sd[i] = value[:, 128:256].astype(BF16)
        reduce_copy(0, i).start()
        reduce_copy(1, i).start()
    weight_2(3)
    weight_1(2)
    weight_3(3)
    weight_ready(3)
    partial(0, block(3))
    partial(1, block(-3))
    for j in range(4):
        reduce_send(0, 2 + j, up_order[j], None if j < 2 else j - 2)
        reduce_send(1, 2 + j, down_order[j], None if j < 2 else j - 2)
    for k in (2, 1):
        weight_2(k)
        if k == 2:
            weight_1(1)
        weight_3(k)
        weight_ready(k)
        partial(0, block(k))
        partial(1, block(-k))
        for j in range(4):
            idx = 4 * (3 - k) + 2 + j
            reduce_send(0, idx, up_order[j], idx - 4)
            reduce_send(1, idx, down_order[j], idx - 4)
    partial(0, z)

    def gather_copy(u, idx, b, r):
        return remote(
            res.at[b, r], res.at[b, r], z_send.at[2 + u], ag_recv.at[u, idx], head=up if u == 0 else down
        )

    loads[4].wait()
    for j, r in enumerate(gather_order):
        i_up = 10 + (2, 3, 0, 1)[j]
        i_down = 10 + j
        reduce_copy(0, i_up).wait_recv()
        reduce_copy(1, i_down).wait_recv()
        value = (pb[0, r] + ru[i_up].astype(F32) + rd[i_down].astype(F32)).astype(BF16)
        cols = pl.ds(pl.multiple_of(r * 128, 128), 128)
        ov[:, cols] = value
        res[z, r] = (value.astype(F32) - tb[:, cols].astype(F32)).astype(BF16)
        gather_copy(0, j, z, r).start()
        gather_copy(1, j, z, r).start()
    out_copy = pltpu.make_async_copy(ov, out_o, out_sem.at[0])
    out_copy.start()

    def residual_block(b, pieces):
        return jnp.concatenate([res[b, r] for r in pieces], axis=1)

    def grads(b, begin=False):
        term = dot(residual_block(b, range(4)), weight_block(b), NN)
        da[...] = term if begin else da[...] + term

    def weight_grads(b):
        row, cols = block_cols(b)
        d_b = dot(residual_block(b, range(4)), att[...], TN).astype(BF16)
        dw[row, cols] = d_b.reshape(2, 2, 128, ROWS)

    def dw_to_core(row, cols, level, slot):
        return remote(
            dw.at[row, cols, sibling], cw.at[level - 1, cols], d_send.at[0], dc_recv.at[slot], seq_2=sibling
        )

    every = pl.ds(0, 4)

    def dw_side(level, toward_right, whole):
        to = right if toward_right else left
        side = 0 if toward_right else 1
        sem = dx_recv.at[4 * (level - 1) + side + (0 if whole else 2)]
        if whole:
            return remote(xs.at[level - 1, to], xr.at[level - 1, side], d_send.at[1], sem, seq_1=to)
        part = first_half if toward_right else second_half
        return remote(
            xs.at[level - 1, across, part], xh.at[level - 1, side], d_send.at[1], sem, seq_1=to
        )

    def dw_1(level):
        row = level_row(level)
        dw_to_core(row, every, level, level - 1).wait_recv()
        for i, to in enumerate((across, right, left, x)):
            xs[level - 1, to] = (
                dw[row, to, c].astype(F32) + cw[level - 1, to].astype(F32)
            ).astype(BF16)
            if i == 0:
                dw_side(level, True, False).start()
                dw_side(level, False, False).start()

    def dw_2(level):
        for side, toward_right in enumerate((True, False)):
            to = right if toward_right else left
            part = first_half if toward_right else second_half
            dw_side(level, toward_right, False).wait_recv()
            value = xs[level - 1, to, part].astype(F32) + xh[level - 1, side].astype(F32)
            xs[level - 1, to, part] = value.astype(BF16)
            dw_side(level, toward_right, True).start()

    def dw_3(level):
        row = level_row(level)
        total = xs[level - 1, x].astype(F32)
        for side, toward_right in enumerate((True, False)):
            dw_side(level, toward_right, True).wait_recv()
            total = total + xr[level - 1, side].astype(F32)

        @pl.when(row == y)
        def _():
            yown[...] = total

        @pl.when(row != y)
        def _():
            ysend[level - 1] = total.astype(BF16)
            d = lax.rem(row - y + 4, 4)
            remote(
                ysend.at[level - 1], yrecv.at[d - 1], d_send.at[2], dy_recv.at[d - 1], seq_0=row
            ).start()

    first_col = 2 * lax.rem(block(4), 2)
    other_col = 2 - first_col
    row3 = level_row(3)
    piece_cols = (
        first_col, first_col + 1, other_col, other_col, other_col + 1, other_col + 1, first_col, first_col + 1
    )
    piece_rows = (row3, row3, row3, row4, row3, row4, row4, row4)
    piece_group = (2, 2, 2, 3, 2, 3, 3, 3)

    def lanes(q):
        return pl.ds(pl.multiple_of(q * 128, 128), 128)

    def along(x_axis, to):
        return {"seq_1": to} if x_axis else {"seq_0": to}

    def piece_to_core(p, count=1):
        cols = pl.ds(piece_cols[p], count)
        return remote(
            dw.at[piece_rows[p], cols, sibling], cw.at[piece_group[p], cols], d_send.at[0],
            dc_recv.at[2 + p], seq_2=sibling,
        )

    def quarter_copy(p, d):
        x_axis = p < 6
        to = lax.rem((x if x_axis else y) + d, 4)
        return remote(
            xs.at[piece_group[p], piece_cols[p], :, lanes(to)], h1.at[p, d - 1], d_send.at[3],
            q1_recv.at[p, d - 1], **along(x_axis, to),
        )

    def quarter_place(p):
        to_col = lax.rem(piece_cols[p] - x + 4, 4)
        to_row = lax.rem(piece_rows[p] - y + 4, 4)
        return (to_row, to_col) if p < 6 else (to_col, to_row)

    def quarter_1(p):
        row, col, group = piece_rows[p], piece_cols[p], piece_group[p]
        if p == 0:
            piece_to_core(0, 2).wait_recv()
        elif p != 1:
            piece_to_core(p).wait_recv()
        xs[group, col] = (dw[row, col, c].astype(F32) + cw[group, col].astype(F32)).astype(BF16)
        for d in (2, 1, 3):
            quarter_copy(p, d).start()

    def quarter_2(p):
        total = xs[piece_group[p], piece_cols[p], :, lanes(x if p < 6 else y)].astype(F32)
        for d in (1, 3, 2):
            quarter_copy(p, d).wait_recv()
            total = total + h1[p, d - 1].astype(F32)
        away, _ = quarter_place(p)
        hk[p] = total

        @pl.when(away != 0)
        def _():
            h2[p] = total.astype(BF16)
            to = piece_rows[p] if p < 6 else piece_cols[p]
            remote(
                h2.at[p], h2r.at[p, away - 1], q2_send.at[p], q2_recv.at[p, away - 1], **along(p >= 6, to)
            ).start()

    def quarter_3(p):
        away, rest = quarter_place(p)

        @pl.when(away == 0)
        def _():
            total = hk[p]
            for d in (1, 3, 2):
                remote(
                    h2r.at[p, d - 1], h2r.at[p, d - 1], q2_send.at[p], q2_recv.at[p, d - 1],
                    **along(p >= 6, lax.rem((x if p >= 6 else y) + d, 4)),
                ).wait_recv()
                total = total + h2r[p, d - 1].astype(F32)

            @pl.when(rest == 0)
            def _():
                yown[:, lanes(x if p < 6 else y)] = total

            @pl.when(rest != 0)
            def _():
                h3[p] = total.astype(BF16)
                group = 0 if p < 6 else 1
                to = piece_cols[p] if p < 6 else piece_rows[p]
                remote(
                    h3.at[p], h3r.at[group, rest - 1], q3_send.at[p], q3_recv.at[group, rest - 1],
                    **along(p < 6, to),
                ).start()

    def quarter_end(group):
        axis_place = x if group == 0 else y
        for d in (1, 3, 2):
            remote(
                h3r.at[group, d - 1], h3r.at[group, d - 1], q3_send.at[0], q3_recv.at[group, d - 1],
                **along(group == 0, lax.rem(axis_place + d, 4)),
            ).wait_recv()
            yown[:, lanes(lax.rem(axis_place - d + 4, 4))] = h3r[group, d - 1].astype(F32)

    grads(z, begin=True)
    weight_grads(z)
    def half_block(b, i):
        row, cols = block_cols(b)
        col = 2 * lax.rem(b, 2) + i
        pieces = residual_block(b, (2 * i, 2 * i + 1))
        d_b = dot(pieces, att[...], TN).astype(BF16)
        dw[row, col] = d_b.reshape(2, 128, ROWS)
        return dot(pieces, wf[row, col].reshape(256, ROWS), NN)

    def both_halves(i):
        @pl.loop(0, 2)
        def _(u):
            da[...] += half_block(block(3 * (2 * u - 1)), i)

    def chunk(k, j):
        r = gather_order[j]
        for u in (0, 1):
            b = block(-k if u == 0 else k)
            gather_copy(u, 4 * (k - 1) + j, b, r).wait_recv()
            if k < 3:
                gather_copy(u, 4 * k + j, b, r).start()
            elif j % 2 == u:
                gather_copy(u, 12 + j // 2, b, r).start()

    for k in (1, 2):
        for j in range(4):
            chunk(k, j)
            if k == 2 and j == 0:
                dw_1(1)
            if k == 2 and j == 2:
                dw_2(1)

        @pl.loop(0, 2)
        def _(u, k=k):
            b = block(k * (2 * u - 1))
            grads(b)
            weight_grads(b)

        dw_to_core(level_row(k), every, k, k - 1).start()
    piece_to_core(0, 2).start()
    chunk(3, 0)
    dw_1(2)
    quarter_1(0)
    quarter_1(1)
    chunk(3, 1)
    both_halves(0)
    piece_to_core(2).start()
    piece_to_core(3).start()
    dw_3(1)
    chunk(3, 2)
    dw_2(2)
    quarter_1(2)
    quarter_1(3)
    quarter_2(0)
    quarter_2(1)
    chunk(3, 3)
    both_halves(1)
    piece_to_core(4).start()
    piece_to_core(5).start()
    dw_3(2)

    b4 = block(4)

    def last_half(i):
        gather_copy(0, 12 + i, b4, gather_order[2 * i]).wait_recv()
        gather_copy(1, 12 + i, b4, gather_order[2 * i + 1]).wait_recv()
        term = dot(residual_block(b4, (2 * i, 2 * i + 1)), wf[row4, first_col + i].reshape(256, ROWS), NN)
        if i == 0:
            da[...] += term
        else:
            dab[...] = (da[...] + term).astype(BF16)

    def last_weight_half(i):
        d_b = dot(residual_block(b4, (2 * i, 2 * i + 1)), att[...], TN).astype(BF16)
        dw[row4, first_col + i] = d_b.reshape(2, 128, ROWS)
        piece_to_core(6 + i).start()

    last_half(0)
    last_weight_half(0)
    quarter_2(2)
    quarter_2(3)
    quarter_1(4)
    quarter_1(5)
    last_half(1)

    for h in range(HEADS):
        cols = head_columns(h)
        tot[1, h] = dot(scaled[:, cols], dab[:, cols], TN)

    scan_begin(1)
    last_weight_half(1)
    scan_x(1)
    quarter_1(6)
    quarter_1(7)
    quarter_3(0)
    quarter_3(1)

    def gradient_pair(start):
        for h in (start, start + 1):
            cols = head_columns(h)
            mixed = jnp.where(causal, dot(dab[:, cols], vb[:, cols], NT), 0.0).astype(BF16)
            g = dot(dab[:, cols], state[0, h], NT) + dot(mixed, kb[:, cols], NN)
            oq[:, cols] = (g * scale).astype(BF16)
            gk_acc[:, cols] = dot(mixed, scaled[:, cols], TN)
            gv_acc[:, cols] = dot(scores[h], dab[:, cols], TN)

    gradient_pair(0)
    quarter_2(4)
    quarter_2(5)
    quarter_3(2)
    quarter_3(3)
    gradient_pair(2)
    scan_y(1, True)
    q_copy = pltpu.make_async_copy(oq, gq_o, out_sem.at[1])
    q_copy.start()
    quarter_2(6)
    quarter_2(7)
    for p in range(4, 8):
        quarter_3(p)
    scan_core(1, True)
    scan_end(1, True)
    out_copy.wait()

    for h in range(HEADS):
        cols = head_columns(h)
        ok[:, cols] = (gk_acc[:, cols] + dot(vb[:, cols], state[1, h], NT)).astype(BF16)
        ov[:, cols] = (gv_acc[:, cols] + dot(kb[:, cols], state[1, h], NN)).astype(BF16)

    k_copy = pltpu.make_async_copy(ok, gk_o, out_sem.at[2])
    k_copy.start()
    v_copy = pltpu.make_async_copy(ov, gv_o, out_sem.at[3])
    v_copy.start()

    in_last = jnp.logical_or(row3 == y, row4 == y)

    @pl.when(jnp.logical_not(in_last))
    def _():
        total = yown[...]
        for d in (1, 3, 2):
            remote(
                yrecv.at[d - 1], yrecv.at[d - 1], d_send.at[2], dy_recv.at[d - 1], seq_0=lax.rem(y + d, 4)
            ).wait_recv()
            total = total + yrecv[d - 1].astype(F32)
        yown[...] = total

    in_second = jnp.logical_and(row4 == y, lax.div(x, 2) == lax.div(first_col, 2))

    @pl.when(jnp.logical_and(in_last, jnp.logical_not(in_second)))
    def _():
        quarter_end(0)

    @pl.when(in_second)
    def _():
        quarter_end(1)

    yown[...] = yown[...] * weight_factor
    w_copy = pltpu.make_async_copy(yown, gw_o, out_sem.at[4])
    w_copy.start()

    wait_bytes(su, z_send.at[0])
    wait_bytes(sd, z_send.at[1])
    wait_bytes(su, z_send.at[2])
    wait_bytes(sd, z_send.at[3])
    wait_bytes(yrecv, w_send.at[0])
    wait_bytes(su.at[pl.ds(0, 12)], w_send.at[1])
    wait_bytes(xs, w_send.at[2])
    wait_bytes(cw, d_send.at[0])
    wait_bytes(su.at[pl.ds(0, 6)], d_send.at[1])

    @pl.when(in_last)
    def _():
        wait_bytes(yrecv.at[pl.ds(0, 2)], d_send.at[2])

    @pl.when(jnp.logical_not(in_last))
    def _():
        wait_bytes(yrecv.at[0], d_send.at[2])

    wait_bytes(su.at[pl.ds(0, 6)], d_send.at[3])
    for p in range(8):
        away, rest = quarter_place(p)

        @pl.when(away != 0)
        def _(p=p):
            wait_bytes(h2.at[p], q2_send.at[p])

        @pl.when(jnp.logical_and(away == 0, rest != 0))
        def _(p=p):
            wait_bytes(h3.at[p], q3_send.at[p])

    for n in (0, 1):
        wait_bytes(loc.at[n], sc_send.at[n, 0])
        wait_bytes(xrc.at[n], sc_send.at[n, 1])
        wait_bytes(yrc.at[n], sc_send.at[n, 2])
        wait_bytes(pfs.at[n], sc_send.at[n, 3])
    for copy in (q_copy, k_copy, v_copy, w_copy):
        copy.wait()


def write_out(*refs):
    sems = refs[-1]
    copies = [pltpu.make_async_copy(refs[i], refs[5 + i], sems.at[i]) for i in range(5)]
    for copy in copies:
        copy.start()
    for copy in copies:
        copy.wait()


def on_device(query_rows, key_rows, value_rows, out_weight, target_rows):
    rows = jax.ShapeDtypeStruct((ROWS, ROWS), BF16)
    total_rows = query_rows.shape[0] * lax.axis_size(SEQ)
    full = (ROWS, ROWS)
    vm = pltpu.VMEM
    scratch = (
        [vm(full, BF16)] * 5
        + [
            vm((4, 4, 2, 128, ROWS), BF16),
            vm(full, BF16),
            vm((2, 4, ROWS, 128), F32),
        ]
        + [vm((14, ROWS, 128), BF16)] * 4
        + [
            vm((8, 4, ROWS, 128), BF16),
            vm(full, F32),
            vm(full, BF16),
            vm((4, 4, 2, 128, ROWS), BF16),
            vm((4, 4, 128, ROWS), BF16),
            vm((4, 4, 128, ROWS), BF16),
            vm((4, 2, 64, ROWS), BF16),
            vm((4, 2, 128, ROWS), BF16),
            vm((4, 128, ROWS), BF16),
            vm((128, ROWS), F32),
            vm((3, 128, ROWS), BF16),
            vm((HEADS, ROWS, ROWS), BF16),
            vm(full, F32),
            vm(full, F32),
        ]
        + [vm(full, BF16)] * 3
        + [
            vm((2, HEADS, DH, DH), F32),
            vm((2, HEADS, DH, DH), BF16),
            vm((2, HEADS, DH, DH), BF16),
            vm((2, 2, DH, DH), BF16),
            vm((2, 3, 2, DH, DH), BF16),
            vm((2, 2, DH, DH), BF16),
            vm((2, 3, 2, DH, DH), BF16),
            vm((2, 2, DH, DH), BF16),
            vm((2, 2, DH, DH), BF16),
            vm((2, 2, DH, DH), F32),
            vm((2, HEADS, DH, DH), BF16),
            vm((8, 3, 128, 128), BF16),
            vm((8, 128, 128), BF16),
            vm((8, 3, 128, 128), BF16),
            vm((8, 128, 128), F32),
            vm((8, 128, 128), BF16),
            vm((2, 3, 128, 128), BF16),
        ]
    )
    dma = pltpu.SemaphoreType.DMA
    scratch += [
        dma((5,)), dma((5,)), dma((2, 14)), dma((2, 14)), dma((4,)), dma((6,)), dma((24,)), dma((16,)),
        dma((3,)), dma((2, 15)), dma((2, 4)), dma((10,)), dma((8,)), dma((3,)), dma((4,)),
        dma((8, 3)), dma((8, 3)), dma((8,)), dma((2, 3)), dma((8,)),
    ]
    anywhere = pl.BlockSpec(memory_space=pl.ANY)

    arguments = (query_rows, key_rows, value_rows, out_weight, target_rows)

    def body(*refs):
        kernel(1.0 / math.sqrt(total_rows), *refs)

    shapes = (rows, rows, rows, rows, jax.ShapeDtypeStruct((128, ROWS), F32))
    results = pl.pallas_call(
        body,
        out_shape=shapes,
        in_specs=[pl.BlockSpec(memory_space=pltpu.HBM)] * 5,
        out_specs=(anywhere,) * 5,
        scratch_shapes=scratch,
        compiler_params=pltpu.CompilerParams(
            collective_id=0, has_side_effects=True, vmem_limit_bytes=48 * 1024 * 1024
        ),
        name="linear_attention",
    )(*(pltpu.with_memory_space_constraint(a, pltpu.HBM) for a in arguments))
    return pl.pallas_call(
        write_out,
        out_shape=shapes,
        in_specs=[anywhere] * 5,
        out_specs=(pl.BlockSpec(memory_space=pltpu.HBM),) * 5,
        scratch_shapes=[dma((5,))],
        compiler_params=pltpu.CompilerParams(vmem_limit_bytes=1024 * 1024),
        name="write_out",
    )(*results)


def solution(mesh):
    torus = Mesh(
        mesh.devices.reshape(4, 4, 2, mesh.shape["head"]), ("seq_0", "seq_1", "seq_2", "head")
    )
    spec = P(SEQ, "head")
    return jax.shard_map(
        on_device, mesh=torus, in_specs=(spec,) * 5, out_specs=(spec,) * 5, check_vma=False
    )
```

```python
import math

import jax
import jax.numpy as jnp
from jax import lax
from jax.experimental import pallas as pl
from jax.experimental.pallas import tpu as pltpu
from jax.sharding import Mesh
from jax.sharding import PartitionSpec as P

DH = 128
ROWS = 512
HEADS = 4
SEQ = ("seq_0", "seq_1", "seq_2")
MESH = pl.DeviceIdType.MESH
F32 = jnp.float32
BF16 = jnp.bfloat16
NT = (((1,), (1,)), ((), ()))
NN = (((1,), (0,)), ((), ()))
TN = (((0,), (0,)), ((), ()))


def dot(a, b, dims):
    return lax.dot_general(a, b, dims, preferred_element_type=F32)


def remote(src, dst, send, recv, **device):
    return pltpu.make_async_remote_copy(
        src_ref=src, dst_ref=dst, send_sem=send, recv_sem=recv, device_id=device, device_id_type=MESH
    )


def wait_bytes(ref, sem):
    pltpu.make_async_copy(ref, ref, sem).wait()


def kernel(
    weight_factor,
    q_in, k_in, v_in, w_in, t_in,
    out_o, gq_o, gk_o, gv_o, gw_o,
    qb, kb, vb, tb, scaled, wf, att, pb, su, sd, ru, rd, res, da, dab, dw, cw, xs, xh, xr, ysend, yown, yrecv,
    scores, gk_acc, gv_acc, oq, ok, ov,
    tot, loc, sib, ct, xrc, rt, yrc, pfs, pfr, px, state, h1, h2, h2r, hk, h3, h3r,
    in_sem, out_sem, rs_recv, ag_recv, z_send, wy_recv, wx_recv, wc_recv, w_send, sc_recv, sc_send,
    dc_recv, dx_recv, dy_recv, d_send, q1_recv, q2_recv, q2_send, q3_recv, q3_send,
):
    y = lax.axis_index("seq_0")
    x = lax.axis_index("seq_1")
    c = lax.axis_index("seq_2")
    z = lax.axis_index("head")
    up = lax.rem(z + 1, 8)
    down = lax.rem(z + 7, 8)
    sibling = 1 - c
    right = lax.rem(x + 1, 4)
    left = lax.rem(x + 3, 4)
    across = lax.rem(x + 2, 4)
    half = lax.div(z, 2)
    turn = 2 * lax.rem(z, 2) - 1
    first_half = pl.ds(0, 64)
    second_half = pl.ds(64, 64)

    def block(k):
        return lax.rem(z + k + 8, 8)

    def level_row(level):
        shift = {1: 0, 2: turn, 3: -turn, 4: 2}[level]
        return lax.rem(half + shift + 4, 4)

    loads = [
        pltpu.make_async_copy(w_in, wf.at[y, x, c], in_sem.at[0]),
        pltpu.make_async_copy(k_in, kb, in_sem.at[1]),
        pltpu.make_async_copy(v_in, vb, in_sem.at[2]),
        pltpu.make_async_copy(q_in, qb, in_sem.at[3]),
        pltpu.make_async_copy(t_in, tb, in_sem.at[4]),
    ]
    for copy in loads:
        copy.start()

    barrier = pltpu.get_barrier_semaphore()
    partners = [{"head": up}, {"head": down}, {"seq_2": sibling}]
    partners += [{"seq_1": lax.rem(x + d, 4)} for d in (1, 2, 3)]
    partners += [{"seq_0": lax.rem(y + d, 4)} for d in (1, 2, 3)]
    for partner in partners:
        pl.semaphore_signal(barrier, inc=1, device_id=partner, device_id_type=MESH)
    pl.semaphore_wait(barrier, len(partners))

    def weight_parts(level):
        return (first_half, second_half) if level >= 3 else (pl.ds(0, 128),)

    def weight_y_copy(level, row, part, d):
        ref = wf.at[row, x, c, weight_parts(level)[part]]
        return remote(ref, ref, w_send.at[0], wy_recv.at[3 * part + d - 1], seq_0=lax.rem(row + d, 4))

    def weight_y(level):
        for d in (2, 3, 1):
            for part in range(len(weight_parts(level))):
                weight_y_copy(level, y, part, d).start()

    def weight_to_core(row, col, slot):
        return remote(
            wf.at[row, col, c], wf.at[row, col, c], w_send.at[2], wc_recv.at[slot], seq_2=sibling
        )

    def weight_side(level, toward_right, part):
        row = level_row(level)
        to, source = (right, left) if toward_right else (left, right)
        side = 0 if toward_right else 1
        if part is None:
            rows = first_half if toward_right else second_half
            sent, got = wf.at[row, source, c, rows], wf.at[row, across, c, rows]
            slot = 4 + side
        else:
            rows = weight_parts(level)[part]
            sent, got = wf.at[row, x, c, rows], wf.at[row, source, c, rows]
            slot = 2 * side + part
        sem = wx_recv.at[6 * (level - 1) + slot]
        return (
            lambda: remote(sent, sent, w_send.at[1], sem, seq_1=to).start(),
            lambda: remote(got, got, w_send.at[1], sem, seq_1=to).wait_recv(),
        )

    def weight_1(level):
        row = level_row(level)
        for part in range(len(weight_parts(level))):

            @pl.when(row != y)
            def _():
                weight_y_copy(level, row, part, lax.rem(y - row + 4, 4)).wait_recv()

            weight_side(level, True, part)[0]()
            weight_side(level, False, part)[0]()
        weight_to_core(row, x, 4 * (level - 1)).start()

    def weight_2(level):
        row = level_row(level)
        last = len(weight_parts(level)) - 1
        weight_side(level, True, 0)[1]()
        weight_side(level, True, None)[0]()
        if last:
            weight_side(level, False, 0)[1]()
        weight_side(level, False, last)[1]()
        weight_side(level, False, None)[0]()
        if last:
            weight_side(level, True, 1)[1]()
        weight_to_core(row, left, 4 * (level - 1) + 1).start()
        weight_to_core(row, right, 4 * (level - 1) + 2).start()

    def weight_3(level):
        row = level_row(level)
        for toward_right in (True, False):
            weight_side(level, toward_right, None)[1]()
        weight_to_core(row, across, 4 * (level - 1) + 3).start()

    def weight_ready(level):
        row = level_row(level)
        for i, col in enumerate((x, left, right, across)):
            slot = 4 * (level - 1) + i
            remote(
                wf.at[row, col, sibling], wf.at[row, col, sibling], w_send.at[2], wc_recv.at[slot],
                seq_2=sibling,
            ).wait_recv()

    loads[0].wait()

    @pl.when(level_row(4) == y)
    def _():
        weight_y(4)

    def head_columns(h):
        return pl.ds(h * DH, DH)

    def scan_begin(n):
        loc[n] = tot[n].astype(BF16)
        remote(loc.at[n], sib.at[n], sc_send.at[n, 0], sc_recv.at[n, 0], seq_2=sibling).start()

    def scan_x_copy(n, i, d):
        return remote(
            ct.at[n, i], xrc.at[n, d - 1, i], sc_send.at[n, 1], sc_recv.at[n, 3 * i + d],
            seq_1=lax.rem(x + d, 4),
        )

    def scan_y_copy(n, i, d):
        return remote(
            rt.at[n, i], yrc.at[n, d - 1, i], sc_send.at[n, 2], sc_recv.at[n, 6 + 3 * i + d],
            seq_0=lax.rem(y + d, 4),
        )

    def scan_core_copy(n, i):
        return remote(
            pfs.at[n, i], pfr.at[n, i], sc_send.at[n, 3], sc_recv.at[n, 13 + i], seq_2=sibling
        )

    def scan_x(n):
        remote(sib.at[n], sib.at[n], sc_send.at[n, 0], sc_recv.at[n, 0], seq_2=sibling).wait_recv()
        for i in (0, 1):
            chip = tot[n, 2 * c + i] + sib[n, 2 * c + i].astype(F32)
            ct[n, i] = chip.astype(BF16)
            for d in (2, 1, 3):
                scan_x_copy(n, i, d).start()

    def scan_y(n, reverse):
        for i in (0, 1):
            total = ct[n, i].astype(F32)
            passed = jnp.zeros((DH, DH), F32)
            for d in (1, 3, 2):
                scan_x_copy(n, i, d).wait_recv()
                piece = xrc[n, d - 1, i].astype(F32)
                total = total + piece
                counts = (d > x) if reverse else (d <= x)
                passed = passed + piece * counts.astype(F32)
            rt[n, i] = total.astype(BF16)
            px[n, i] = passed
            for d in (2, 1, 3):
                scan_y_copy(n, i, d).start()

    def scan_core(n, reverse):
        for i in (0, 1):
            passed = px[n, i]
            for d in (1, 3, 2):
                scan_y_copy(n, i, d).wait_recv()
                counts = (d > y) if reverse else (d <= y)
                passed = passed + yrc[n, d - 1, i].astype(F32) * counts.astype(F32)
            px[n, i] = passed
            pfs[n, i] = passed.astype(BF16)
            scan_core_copy(n, i).start()

    def scan_end(n, reverse):
        own_core = (c == 0) if reverse else (c == 1)
        factor = own_core.astype(F32)
        for i in (0, 1):
            ours, theirs = 2 * c + i, 2 * sibling + i
            state[n, ours] = (px[n, i] + sib[n, ours].astype(F32) * factor).astype(BF16)
            scan_core_copy(n, i).wait_recv()
            state[n, theirs] = (pfr[n, i].astype(F32) + sib[n, theirs].astype(F32) * factor).astype(BF16)

    loads[1].wait()
    loads[2].wait()

    for h in range(HEADS):
        cols = head_columns(h)
        tot[0, h] = dot(kb[:, cols], vb[:, cols], TN)

    scan_begin(0)

    @pl.when(level_row(3) == y)
    def _():
        weight_y(3)

    first = lax.rem((y * 4 + x) * 2 + c, 32) * ROWS
    positions = (first + lax.broadcasted_iota(jnp.int32, (ROWS, 1), 0) + 1).astype(F32)
    scale = lax.rsqrt(F32(DH) * positions)
    loads[3].wait()
    scaled[...] = (qb[...].astype(F32) * scale).astype(BF16)
    scan_x(0)

    causal = lax.broadcasted_iota(jnp.int32, (ROWS, ROWS), 0) >= lax.broadcasted_iota(
        jnp.int32, (ROWS, ROWS), 1
    )

    for h in range(HEADS):
        cols = head_columns(h)
        s = dot(scaled[:, cols], kb[:, cols], NT)
        scores[h] = jnp.where(causal, s, 0.0).astype(BF16)

    weight_1(4)

    for h in range(HEADS):
        cols = head_columns(h)
        gk_acc[:, cols] = dot(scores[h], vb[:, cols], NN)

    scan_y(0, False)

    weight_2(4)
    weight_1(3)
    scan_core(0, False)

    @pl.when(level_row(2) == y)
    def _():
        weight_y(2)

    weight_3(4)
    scan_end(0, False)

    for h in range(HEADS):
        cols = head_columns(h)
        att[:, cols] = (dot(scaled[:, cols], state[0, h], NN) + gk_acc[:, cols]).astype(BF16)

    up_order = (2 + c, 3 - c, c, 1 - c)
    down_order = (c, 1 - c, 2 + c, 3 - c)
    gather_order = (c, 1 - c, 2 + c, 3 - c)

    def block_cols(b):
        return lax.div(b, 2), pl.ds(2 * lax.rem(b, 2), 2)

    def weight_block(b):
        row, cols = block_cols(b)
        return wf[row, cols].reshape(ROWS, ROWS)

    def partial(u, b):
        value = dot(att[...], weight_block(b), NT)
        for r in range(4):
            pb[u, r] = value[:, r * 128 : (r + 1) * 128]

    def reduce_copy(u, idx):
        src, dst = (su, ru) if u == 0 else (sd, rd)
        return remote(
            src.at[idx], dst.at[idx], z_send.at[u], rs_recv.at[u, idx], head=up if u == 0 else down
        )

    def reduce_send(u, idx, r, received):
        src, dst = (su, ru) if u == 0 else (sd, rd)
        value = pb[u, r]
        if received is not None:
            reduce_copy(u, received).wait_recv()
            value = value + dst[received].astype(F32)
        src[idx] = value.astype(BF16)
        reduce_copy(u, idx).start()

    row4, cols4 = block_cols(block(4))
    for i, core in enumerate((c, sibling)):
        if i == 1:
            weight_ready(4)
        value = dot(att[...], wf[row4, cols4, core].reshape(256, ROWS), NT)
        su[i] = value[:, 0:128].astype(BF16)
        sd[i] = value[:, 128:256].astype(BF16)
        reduce_copy(0, i).start()
        reduce_copy(1, i).start()
    weight_2(3)
    weight_3(3)
    weight_1(2)

    @pl.when(level_row(1) == y)
    def _():
        weight_y(1)

    weight_ready(3)
    partial(0, block(3))
    partial(1, block(-3))
    for j in range(4):
        reduce_send(0, 2 + j, up_order[j], None if j < 2 else j - 2)
        reduce_send(1, 2 + j, down_order[j], None if j < 2 else j - 2)
    for k in (2, 1):
        weight_2(k)
        weight_3(k)
        weight_ready(k)
        if k == 2:
            weight_1(1)
        partial(0, block(k))
        partial(1, block(-k))
        for j in range(4):
            idx = 4 * (3 - k) + 2 + j
            reduce_send(0, idx, up_order[j], idx - 4)
            reduce_send(1, idx, down_order[j], idx - 4)
    partial(0, z)

    def gather_copy(u, idx, b, r):
        return remote(
            res.at[b, r], res.at[b, r], z_send.at[2 + u], ag_recv.at[u, idx], head=up if u == 0 else down
        )

    loads[4].wait()
    for j, r in enumerate(gather_order):
        i_up = 10 + (2, 3, 0, 1)[j]
        i_down = 10 + j
        reduce_copy(0, i_up).wait_recv()
        reduce_copy(1, i_down).wait_recv()
        value = (pb[0, r] + ru[i_up].astype(F32) + rd[i_down].astype(F32)).astype(BF16)
        cols = pl.ds(pl.multiple_of(r * 128, 128), 128)
        ov[:, cols] = value
        res[z, r] = (value.astype(F32) - tb[:, cols].astype(F32)).astype(BF16)
        gather_copy(0, j, z, r).start()
        gather_copy(1, j, z, r).start()
    out_copy = pltpu.make_async_copy(ov, out_o, out_sem.at[0])
    out_copy.start()

    def residual_block(b, pieces):
        return jnp.concatenate([res[b, r] for r in pieces], axis=1)

    def grads(b, begin=False):
        term = dot(residual_block(b, range(4)), weight_block(b), NN)
        da[...] = term if begin else da[...] + term

    def weight_grads(b):
        row, cols = block_cols(b)
        d_b = dot(residual_block(b, range(4)), att[...], TN).astype(BF16)
        dw[row, cols] = d_b.reshape(2, 2, 128, ROWS)

    def dw_to_core(row, cols, level, slot):
        return remote(
            dw.at[row, cols, sibling], cw.at[level - 1, cols], d_send.at[0], dc_recv.at[slot], seq_2=sibling
        )

    every = pl.ds(0, 4)

    def dw_side(level, toward_right, whole):
        to = right if toward_right else left
        side = 0 if toward_right else 1
        sem = dx_recv.at[4 * (level - 1) + side + (0 if whole else 2)]
        if whole:
            return remote(xs.at[level - 1, to], xr.at[level - 1, side], d_send.at[1], sem, seq_1=to)
        part = first_half if toward_right else second_half
        return remote(
            xs.at[level - 1, across, part], xh.at[level - 1, side], d_send.at[1], sem, seq_1=to
        )

    def dw_1(level):
        row = level_row(level)
        dw_to_core(row, every, level, level - 1).wait_recv()
        for i, to in enumerate((across, right, left, x)):
            xs[level - 1, to] = (
                dw[row, to, c].astype(F32) + cw[level - 1, to].astype(F32)
            ).astype(BF16)
            if i == 0:
                dw_side(level, True, False).start()
                dw_side(level, False, False).start()

    def dw_2(level):
        for side, toward_right in enumerate((True, False)):
            to = right if toward_right else left
            part = first_half if toward_right else second_half
            dw_side(level, toward_right, False).wait_recv()
            value = xs[level - 1, to, part].astype(F32) + xh[level - 1, side].astype(F32)
            xs[level - 1, to, part] = value.astype(BF16)
            dw_side(level, toward_right, True).start()

    def dw_3(level):
        row = level_row(level)
        total = xs[level - 1, x].astype(F32)
        for side, toward_right in enumerate((True, False)):
            dw_side(level, toward_right, True).wait_recv()
            total = total + xr[level - 1, side].astype(F32)

        @pl.when(row == y)
        def _():
            yown[...] = total

        @pl.when(row != y)
        def _():
            ysend[level - 1] = total.astype(BF16)
            d = lax.rem(row - y + 4, 4)
            remote(
                ysend.at[level - 1], yrecv.at[d - 1], d_send.at[2], dy_recv.at[d - 1], seq_0=row
            ).start()

    first_col = 2 * lax.rem(block(4), 2)
    other_col = 2 - first_col
    row3 = level_row(3)
    piece_cols = (
        first_col, first_col + 1, other_col, other_col, other_col + 1, other_col + 1, first_col, first_col + 1
    )
    piece_rows = (row3, row3, row3, row4, row3, row4, row4, row4)
    piece_group = (2, 2, 2, 3, 2, 3, 3, 3)

    def lanes(q):
        return pl.ds(pl.multiple_of(q * 128, 128), 128)

    def along(x_axis, to):
        return {"seq_1": to} if x_axis else {"seq_0": to}

    def piece_to_core(p, count=1):
        cols = pl.ds(piece_cols[p], count)
        return remote(
            dw.at[piece_rows[p], cols, sibling], cw.at[piece_group[p], cols], d_send.at[0],
            dc_recv.at[2 + p], seq_2=sibling,
        )

    def quarter_copy(p, d):
        x_axis = p < 6
        to = lax.rem((x if x_axis else y) + d, 4)
        return remote(
            xs.at[piece_group[p], piece_cols[p], :, lanes(to)], h1.at[p, d - 1], d_send.at[3],
            q1_recv.at[p, d - 1], **along(x_axis, to),
        )

    def quarter_place(p):
        to_col = lax.rem(piece_cols[p] - x + 4, 4)
        to_row = lax.rem(piece_rows[p] - y + 4, 4)
        return (to_row, to_col) if p < 6 else (to_col, to_row)

    def quarter_1(p):
        row, col, group = piece_rows[p], piece_cols[p], piece_group[p]
        if p == 0:
            piece_to_core(0, 2).wait_recv()
        elif p != 1:
            piece_to_core(p).wait_recv()
        xs[group, col] = (dw[row, col, c].astype(F32) + cw[group, col].astype(F32)).astype(BF16)
        for d in (2, 1, 3):
            quarter_copy(p, d).start()

    def quarter_2(p):
        total = xs[piece_group[p], piece_cols[p], :, lanes(x if p < 6 else y)].astype(F32)
        for d in (1, 3, 2):
            quarter_copy(p, d).wait_recv()
            total = total + h1[p, d - 1].astype(F32)
        away, _ = quarter_place(p)
        hk[p] = total

        @pl.when(away != 0)
        def _():
            h2[p] = total.astype(BF16)
            to = piece_rows[p] if p < 6 else piece_cols[p]
            remote(
                h2.at[p], h2r.at[p, away - 1], q2_send.at[p], q2_recv.at[p, away - 1], **along(p >= 6, to)
            ).start()

    def quarter_3(p):
        away, rest = quarter_place(p)

        @pl.when(away == 0)
        def _():
            total = hk[p]
            for d in (1, 3, 2):
                remote(
                    h2r.at[p, d - 1], h2r.at[p, d - 1], q2_send.at[p], q2_recv.at[p, d - 1],
                    **along(p >= 6, lax.rem((x if p >= 6 else y) + d, 4)),
                ).wait_recv()
                total = total + h2r[p, d - 1].astype(F32)

            @pl.when(rest == 0)
            def _():
                yown[:, lanes(x if p < 6 else y)] = total

            @pl.when(rest != 0)
            def _():
                h3[p] = total.astype(BF16)
                group = 0 if p < 6 else 1
                to = piece_cols[p] if p < 6 else piece_rows[p]
                remote(
                    h3.at[p], h3r.at[group, rest - 1], q3_send.at[p], q3_recv.at[group, rest - 1],
                    **along(p < 6, to),
                ).start()

    def quarter_end(group):
        axis_place = x if group == 0 else y
        for d in (1, 3, 2):
            remote(
                h3r.at[group, d - 1], h3r.at[group, d - 1], q3_send.at[0], q3_recv.at[group, d - 1],
                **along(group == 0, lax.rem(axis_place + d, 4)),
            ).wait_recv()
            yown[:, lanes(lax.rem(axis_place - d + 4, 4))] = h3r[group, d - 1].astype(F32)

    grads(z, begin=True)
    weight_grads(z)
    def half_block(b, i):
        row, cols = block_cols(b)
        col = 2 * lax.rem(b, 2) + i
        pieces = residual_block(b, (2 * i, 2 * i + 1))
        d_b = dot(pieces, att[...], TN).astype(BF16)
        dw[row, col] = d_b.reshape(2, 128, ROWS)
        return dot(pieces, wf[row, col].reshape(256, ROWS), NN)

    def both_halves(i):
        @pl.loop(0, 2)
        def _(u):
            da[...] += half_block(block(3 * (2 * u - 1)), i)

    def chunk(k, j):
        r = gather_order[j]
        for u in (0, 1):
            b = block(-k if u == 0 else k)
            gather_copy(u, 4 * (k - 1) + j, b, r).wait_recv()
            if k < 3:
                gather_copy(u, 4 * k + j, b, r).start()
            elif j % 2 == u:
                gather_copy(u, 12 + j // 2, b, r).start()

    for k in (1, 2):
        for j in range(4):
            chunk(k, j)
            if k == 2 and j == 0:
                dw_1(1)
            if k == 2 and j == 2:
                dw_2(1)

        @pl.loop(0, 2)
        def _(u, k=k):
            b = block(k * (2 * u - 1))
            grads(b)
            weight_grads(b)

        dw_to_core(level_row(k), every, k, k - 1).start()
    piece_to_core(0, 2).start()
    chunk(3, 0)
    dw_1(2)
    quarter_1(0)
    quarter_1(1)
    chunk(3, 1)
    both_halves(0)
    piece_to_core(2).start()
    piece_to_core(3).start()
    dw_3(1)
    chunk(3, 2)
    dw_2(2)
    quarter_1(2)
    quarter_1(3)
    quarter_2(0)
    quarter_2(1)
    chunk(3, 3)
    both_halves(1)
    piece_to_core(4).start()
    piece_to_core(5).start()

    b4 = block(4)

    def last_half(i):
        gather_copy(0, 12 + i, b4, gather_order[2 * i]).wait_recv()
        gather_copy(1, 12 + i, b4, gather_order[2 * i + 1]).wait_recv()
        term = dot(residual_block(b4, (2 * i, 2 * i + 1)), wf[row4, first_col + i].reshape(256, ROWS), NN)
        if i == 0:
            da[...] += term
        else:
            dab[...] = (da[...] + term).astype(BF16)

    def last_weight_half(i):
        d_b = dot(residual_block(b4, (2 * i, 2 * i + 1)), att[...], TN).astype(BF16)
        dw[row4, first_col + i] = d_b.reshape(2, 128, ROWS)
        piece_to_core(6 + i).start()

    last_half(0)
    last_weight_half(0)
    quarter_1(4)
    quarter_1(5)
    dw_3(2)
    last_half(1)

    for h in range(HEADS):
        cols = head_columns(h)
        tot[1, h] = dot(scaled[:, cols], dab[:, cols], TN)

    scan_begin(1)
    last_weight_half(1)
    quarter_2(2)
    quarter_2(3)
    scan_x(1)
    quarter_1(6)
    quarter_1(7)
    quarter_3(0)
    quarter_3(1)

    def gradient_pair(start):
        for h in (start, start + 1):
            cols = head_columns(h)
            mixed = jnp.where(causal, dot(dab[:, cols], vb[:, cols], NT), 0.0).astype(BF16)
            g = dot(dab[:, cols], state[0, h], NT) + dot(mixed, kb[:, cols], NN)
            oq[:, cols] = (g * scale).astype(BF16)
            gk_acc[:, cols] = dot(mixed, scaled[:, cols], TN)
            gv_acc[:, cols] = dot(scores[h], dab[:, cols], TN)

    gradient_pair(0)
    quarter_2(4)
    quarter_2(5)
    quarter_3(2)
    quarter_3(3)
    gradient_pair(2)
    scan_y(1, True)
    q_copy = pltpu.make_async_copy(oq, gq_o, out_sem.at[1])
    q_copy.start()
    quarter_2(6)
    quarter_2(7)
    quarter_3(4)
    quarter_3(5)
    scan_core(1, True)
    quarter_3(6)
    quarter_3(7)
    scan_end(1, True)
    out_copy.wait()

    for h in range(HEADS):
        cols = head_columns(h)
        ok[:, cols] = (gk_acc[:, cols] + dot(vb[:, cols], state[1, h], NT)).astype(BF16)
        ov[:, cols] = (gv_acc[:, cols] + dot(kb[:, cols], state[1, h], NN)).astype(BF16)

    k_copy = pltpu.make_async_copy(ok, gk_o, out_sem.at[2])
    k_copy.start()
    v_copy = pltpu.make_async_copy(ov, gv_o, out_sem.at[3])
    v_copy.start()

    in_last = jnp.logical_or(row3 == y, row4 == y)

    @pl.when(jnp.logical_not(in_last))
    def _():
        total = yown[...]
        for d in (1, 3, 2):
            remote(
                yrecv.at[d - 1], yrecv.at[d - 1], d_send.at[2], dy_recv.at[d - 1], seq_0=lax.rem(y + d, 4)
            ).wait_recv()
            total = total + yrecv[d - 1].astype(F32)
        yown[...] = total

    in_second = jnp.logical_and(row4 == y, lax.div(x, 2) == lax.div(first_col, 2))

    @pl.when(jnp.logical_and(in_last, jnp.logical_not(in_second)))
    def _():
        quarter_end(0)

    @pl.when(in_second)
    def _():
        quarter_end(1)

    yown[...] = yown[...] * weight_factor
    w_copy = pltpu.make_async_copy(yown, gw_o, out_sem.at[4])
    w_copy.start()

    wait_bytes(su, z_send.at[0])
    wait_bytes(sd, z_send.at[1])
    wait_bytes(su, z_send.at[2])
    wait_bytes(sd, z_send.at[3])
    wait_bytes(yrecv, w_send.at[0])
    wait_bytes(su.at[pl.ds(0, 12)], w_send.at[1])
    wait_bytes(xs, w_send.at[2])
    wait_bytes(cw, d_send.at[0])
    wait_bytes(su.at[pl.ds(0, 6)], d_send.at[1])

    @pl.when(in_last)
    def _():
        wait_bytes(yrecv.at[pl.ds(0, 2)], d_send.at[2])

    @pl.when(jnp.logical_not(in_last))
    def _():
        wait_bytes(yrecv.at[0], d_send.at[2])

    wait_bytes(su.at[pl.ds(0, 6)], d_send.at[3])
    for p in range(8):
        away, rest = quarter_place(p)

        @pl.when(away != 0)
        def _(p=p):
            wait_bytes(h2.at[p], q2_send.at[p])

        @pl.when(jnp.logical_and(away == 0, rest != 0))
        def _(p=p):
            wait_bytes(h3.at[p], q3_send.at[p])

    for n in (0, 1):
        wait_bytes(loc.at[n], sc_send.at[n, 0])
        wait_bytes(xrc.at[n], sc_send.at[n, 1])
        wait_bytes(yrc.at[n], sc_send.at[n, 2])
        wait_bytes(pfs.at[n], sc_send.at[n, 3])
    for copy in (q_copy, k_copy, v_copy, w_copy):
        copy.wait()


def write_out(*refs):
    sems = refs[-1]
    copies = [pltpu.make_async_copy(refs[i], refs[5 + i], sems.at[i]) for i in range(5)]
    for copy in copies:
        copy.start()
    for copy in copies:
        copy.wait()


def on_device(query_rows, key_rows, value_rows, out_weight, target_rows):
    rows = jax.ShapeDtypeStruct((ROWS, ROWS), BF16)
    total_rows = query_rows.shape[0] * lax.axis_size(SEQ)
    full = (ROWS, ROWS)
    vm = pltpu.VMEM
    scratch = (
        [vm(full, BF16)] * 5
        + [
            vm((4, 4, 2, 128, ROWS), BF16),
            vm(full, BF16),
            vm((2, 4, ROWS, 128), F32),
        ]
        + [vm((14, ROWS, 128), BF16)] * 4
        + [
            vm((8, 4, ROWS, 128), BF16),
            vm(full, F32),
            vm(full, BF16),
            vm((4, 4, 2, 128, ROWS), BF16),
            vm((4, 4, 128, ROWS), BF16),
            vm((4, 4, 128, ROWS), BF16),
            vm((4, 2, 64, ROWS), BF16),
            vm((4, 2, 128, ROWS), BF16),
            vm((4, 128, ROWS), BF16),
            vm((128, ROWS), F32),
            vm((3, 128, ROWS), BF16),
            vm((HEADS, ROWS, ROWS), BF16),
            vm(full, F32),
            vm(full, F32),
        ]
        + [vm(full, BF16)] * 3
        + [
            vm((2, HEADS, DH, DH), F32),
            vm((2, HEADS, DH, DH), BF16),
            vm((2, HEADS, DH, DH), BF16),
            vm((2, 2, DH, DH), BF16),
            vm((2, 3, 2, DH, DH), BF16),
            vm((2, 2, DH, DH), BF16),
            vm((2, 3, 2, DH, DH), BF16),
            vm((2, 2, DH, DH), BF16),
            vm((2, 2, DH, DH), BF16),
            vm((2, 2, DH, DH), F32),
            vm((2, HEADS, DH, DH), BF16),
            vm((8, 3, 128, 128), BF16),
            vm((8, 128, 128), BF16),
            vm((8, 3, 128, 128), BF16),
            vm((8, 128, 128), F32),
            vm((8, 128, 128), BF16),
            vm((2, 3, 128, 128), BF16),
        ]
    )
    dma = pltpu.SemaphoreType.DMA
    scratch += [
        dma((5,)), dma((5,)), dma((2, 14)), dma((2, 14)), dma((4,)), dma((6,)), dma((24,)), dma((16,)),
        dma((3,)), dma((2, 15)), dma((2, 4)), dma((10,)), dma((8,)), dma((3,)), dma((4,)),
        dma((8, 3)), dma((8, 3)), dma((8,)), dma((2, 3)), dma((8,)),
    ]
    anywhere = pl.BlockSpec(memory_space=pl.ANY)

    arguments = (query_rows, key_rows, value_rows, out_weight, target_rows)

    def body(*refs):
        kernel(1.0 / math.sqrt(total_rows), *refs)

    shapes = (rows, rows, rows, rows, jax.ShapeDtypeStruct((128, ROWS), F32))
    results = pl.pallas_call(
        body,
        out_shape=shapes,
        in_specs=[pl.BlockSpec(memory_space=pltpu.HBM)] * 5,
        out_specs=(anywhere,) * 5,
        scratch_shapes=scratch,
        compiler_params=pltpu.CompilerParams(
            collective_id=0, has_side_effects=True, vmem_limit_bytes=48 * 1024 * 1024
        ),
        name="linear_attention",
    )(*(pltpu.with_memory_space_constraint(a, pltpu.HBM) for a in arguments))
    return pl.pallas_call(
        write_out,
        out_shape=shapes,
        in_specs=[anywhere] * 5,
        out_specs=(pl.BlockSpec(memory_space=pltpu.HBM),) * 5,
        scratch_shapes=[dma((5,))],
        compiler_params=pltpu.CompilerParams(vmem_limit_bytes=1024 * 1024),
        name="write_out",
    )(*results)


def solution(mesh):
    torus = Mesh(
        mesh.devices.reshape(4, 4, 2, mesh.shape["head"]), ("seq_0", "seq_1", "seq_2", "head")
    )
    spec = P(SEQ, "head")
    return jax.shard_map(
        on_device, mesh=torus, in_specs=(spec,) * 5, out_specs=(spec,) * 5, check_vma=False
    )
```

```python
import math

import jax
import jax.numpy as jnp
from jax import lax
from jax.experimental import pallas as pl
from jax.experimental.pallas import tpu as pltpu
from jax.sharding import Mesh
from jax.sharding import PartitionSpec as P

DH = 128
ROWS = 512
HEADS = 4
SEQ = ("seq_0", "seq_1", "seq_2")
MESH = pl.DeviceIdType.MESH
F32 = jnp.float32
BF16 = jnp.bfloat16
NT = (((1,), (1,)), ((), ()))
NN = (((1,), (0,)), ((), ()))
TN = (((0,), (0,)), ((), ()))


def dot(a, b, dims):
    return lax.dot_general(a, b, dims, preferred_element_type=F32)


def remote(src, dst, send, recv, **device):
    return pltpu.make_async_remote_copy(
        src_ref=src, dst_ref=dst, send_sem=send, recv_sem=recv, device_id=device, device_id_type=MESH
    )


def wait_bytes(ref, sem):
    pltpu.make_async_copy(ref, ref, sem).wait()


def kernel(
    weight_factor,
    q_in, k_in, v_in, w_in, t_in,
    out_o, gq_o, gk_o, gv_o, gw_o,
    qb, kb, vb, tb, scaled, wf, att, pb, su, sd, ru, rd, res, da, dab, dw, cw, xs, xh, xr, ysend, yown, yrecv,
    scores, gk_acc, gv_acc, oq, ok, ov,
    tot, loc, sib, ct, xrc, rt, yrc, pfs, pfr, px, state, h1, h2, h2r, hk, h3, h3r,
    in_sem, out_sem, rs_recv, ag_recv, z_send, wy_recv, wx_recv, wc_recv, w_send, sc_recv, sc_send,
    dc_recv, dx_recv, dy_recv, d_send, q1_recv, q2_recv, q2_send, q3_recv, q3_send,
):
    y = lax.axis_index("seq_0")
    x = lax.axis_index("seq_1")
    c = lax.axis_index("seq_2")
    z = lax.axis_index("head")
    up = lax.rem(z + 1, 8)
    down = lax.rem(z + 7, 8)
    sibling = 1 - c
    right = lax.rem(x + 1, 4)
    left = lax.rem(x + 3, 4)
    across = lax.rem(x + 2, 4)
    half = lax.div(z, 2)
    turn = 2 * lax.rem(z, 2) - 1
    first_half = pl.ds(0, 64)
    second_half = pl.ds(64, 64)

    def block(k):
        return lax.rem(z + k + 8, 8)

    def level_row(level):
        shift = {1: 0, 2: turn, 3: -turn, 4: 2}[level]
        return lax.rem(half + shift + 4, 4)

    loads = [
        pltpu.make_async_copy(w_in, wf.at[y, x, c], in_sem.at[0]),
        pltpu.make_async_copy(k_in, kb, in_sem.at[1]),
        pltpu.make_async_copy(v_in, vb, in_sem.at[2]),
        pltpu.make_async_copy(q_in, qb, in_sem.at[3]),
        pltpu.make_async_copy(t_in, tb, in_sem.at[4]),
    ]
    for copy in loads:
        copy.start()

    barrier = pltpu.get_barrier_semaphore()
    partners = [{"head": up}, {"head": down}, {"seq_2": sibling}]
    partners += [{"seq_1": lax.rem(x + d, 4)} for d in (1, 2, 3)]
    partners += [{"seq_0": lax.rem(y + d, 4)} for d in (1, 2, 3)]
    for partner in partners:
        pl.semaphore_signal(barrier, inc=1, device_id=partner, device_id_type=MESH)
    pl.semaphore_wait(barrier, len(partners))

    def weight_parts(level):
        return (first_half, second_half) if level >= 3 else (pl.ds(0, 128),)

    def weight_y_copy(level, row, part, d):
        ref = wf.at[row, x, c, weight_parts(level)[part]]
        return remote(ref, ref, w_send.at[0], wy_recv.at[3 * part + d - 1], seq_0=lax.rem(row + d, 4))

    def weight_y(level):
        for d in (2, 3, 1):
            for part in range(len(weight_parts(level))):
                weight_y_copy(level, y, part, d).start()

    def weight_to_core(row, col, slot):
        return remote(
            wf.at[row, col, c], wf.at[row, col, c], w_send.at[2], wc_recv.at[slot], seq_2=sibling
        )

    def weight_side(level, toward_right, part):
        row = level_row(level)
        to, source = (right, left) if toward_right else (left, right)
        side = 0 if toward_right else 1
        if part is None:
            rows = first_half if toward_right else second_half
            sent, got = wf.at[row, source, c, rows], wf.at[row, across, c, rows]
            slot = 4 + side
        else:
            rows = weight_parts(level)[part]
            sent, got = wf.at[row, x, c, rows], wf.at[row, source, c, rows]
            slot = 2 * side + part
        sem = wx_recv.at[6 * (level - 1) + slot]
        return (
            lambda: remote(sent, sent, w_send.at[1], sem, seq_1=to).start(),
            lambda: remote(got, got, w_send.at[1], sem, seq_1=to).wait_recv(),
        )

    def weight_1(level):
        row = level_row(level)
        for part in range(len(weight_parts(level))):

            @pl.when(row != y)
            def _():
                weight_y_copy(level, row, part, lax.rem(y - row + 4, 4)).wait_recv()

            weight_side(level, True, part)[0]()
            weight_side(level, False, part)[0]()
        weight_to_core(row, x, 4 * (level - 1)).start()

    def weight_2(level):
        row = level_row(level)
        last = len(weight_parts(level)) - 1
        weight_side(level, True, 0)[1]()
        weight_side(level, True, None)[0]()
        if last:
            weight_side(level, False, 0)[1]()
        weight_side(level, False, last)[1]()
        weight_side(level, False, None)[0]()
        if last:
            weight_side(level, True, 1)[1]()
        weight_to_core(row, left, 4 * (level - 1) + 1).start()
        weight_to_core(row, right, 4 * (level - 1) + 2).start()

    def weight_3(level):
        row = level_row(level)
        for toward_right in (True, False):
            weight_side(level, toward_right, None)[1]()
        weight_to_core(row, across, 4 * (level - 1) + 3).start()

    def weight_ready(level):
        row = level_row(level)
        for i, col in enumerate((x, left, right, across)):
            slot = 4 * (level - 1) + i
            remote(
                wf.at[row, col, sibling], wf.at[row, col, sibling], w_send.at[2], wc_recv.at[slot],
                seq_2=sibling,
            ).wait_recv()

    loads[0].wait()

    @pl.when(level_row(4) == y)
    def _():
        weight_y(4)

    def head_columns(h):
        return pl.ds(h * DH, DH)

    def scan_begin(n):
        loc[n] = tot[n].astype(BF16)
        remote(loc.at[n], sib.at[n], sc_send.at[n, 0], sc_recv.at[n, 0], seq_2=sibling).start()

    def scan_x_copy(n, i, d):
        return remote(
            ct.at[n, i], xrc.at[n, d - 1, i], sc_send.at[n, 1], sc_recv.at[n, 3 * i + d],
            seq_1=lax.rem(x + d, 4),
        )

    def scan_y_copy(n, i, d):
        return remote(
            rt.at[n, i], yrc.at[n, d - 1, i], sc_send.at[n, 2], sc_recv.at[n, 6 + 3 * i + d],
            seq_0=lax.rem(y + d, 4),
        )

    def scan_core_copy(n, i):
        return remote(
            pfs.at[n, i], pfr.at[n, i], sc_send.at[n, 3], sc_recv.at[n, 13 + i], seq_2=sibling
        )

    def scan_x(n):
        remote(sib.at[n], sib.at[n], sc_send.at[n, 0], sc_recv.at[n, 0], seq_2=sibling).wait_recv()
        for i in (0, 1):
            chip = tot[n, 2 * c + i] + sib[n, 2 * c + i].astype(F32)
            ct[n, i] = chip.astype(BF16)
            for d in (2, 1, 3):
                scan_x_copy(n, i, d).start()

    def scan_y(n, reverse):
        for i in (0, 1):
            total = ct[n, i].astype(F32)
            passed = jnp.zeros((DH, DH), F32)
            for d in (1, 3, 2):
                scan_x_copy(n, i, d).wait_recv()
                piece = xrc[n, d - 1, i].astype(F32)
                total = total + piece
                counts = (d > x) if reverse else (d <= x)
                passed = passed + piece * counts.astype(F32)
            rt[n, i] = total.astype(BF16)
            px[n, i] = passed
            for d in (2, 1, 3):
                scan_y_copy(n, i, d).start()

    def scan_core(n, reverse):
        for i in (0, 1):
            passed = px[n, i]
            for d in (1, 3, 2):
                scan_y_copy(n, i, d).wait_recv()
                counts = (d > y) if reverse else (d <= y)
                passed = passed + yrc[n, d - 1, i].astype(F32) * counts.astype(F32)
            px[n, i] = passed
            pfs[n, i] = passed.astype(BF16)
            scan_core_copy(n, i).start()

    def scan_end(n, reverse):
        own_core = (c == 0) if reverse else (c == 1)
        factor = own_core.astype(F32)
        for i in (0, 1):
            ours, theirs = 2 * c + i, 2 * sibling + i
            state[n, ours] = (px[n, i] + sib[n, ours].astype(F32) * factor).astype(BF16)
            scan_core_copy(n, i).wait_recv()
            state[n, theirs] = (pfr[n, i].astype(F32) + sib[n, theirs].astype(F32) * factor).astype(BF16)

    loads[1].wait()
    loads[2].wait()

    for h in range(HEADS):
        cols = head_columns(h)
        tot[0, h] = dot(kb[:, cols], vb[:, cols], TN)

    scan_begin(0)

    @pl.when(level_row(3) == y)
    def _():
        weight_y(3)

    first = lax.rem((y * 4 + x) * 2 + c, 32) * ROWS
    positions = (first + lax.broadcasted_iota(jnp.int32, (ROWS, 1), 0) + 1).astype(F32)
    scale = lax.rsqrt(F32(DH) * positions)
    loads[3].wait()
    scaled[...] = (qb[...].astype(F32) * scale).astype(BF16)
    scan_x(0)

    causal = lax.broadcasted_iota(jnp.int32, (ROWS, ROWS), 0) >= lax.broadcasted_iota(
        jnp.int32, (ROWS, ROWS), 1
    )

    for h in range(HEADS):
        cols = head_columns(h)
        s = dot(scaled[:, cols], kb[:, cols], NT)
        scores[h] = jnp.where(causal, s, 0.0).astype(BF16)

    weight_1(4)

    for h in range(HEADS):
        cols = head_columns(h)
        gk_acc[:, cols] = dot(scores[h], vb[:, cols], NN)

    scan_y(0, False)

    weight_2(4)
    weight_1(3)
    scan_core(0, False)

    @pl.when(level_row(2) == y)
    def _():
        weight_y(2)

    weight_3(4)
    scan_end(0, False)

    for h in range(HEADS):
        cols = head_columns(h)
        att[:, cols] = (dot(scaled[:, cols], state[0, h], NN) + gk_acc[:, cols]).astype(BF16)

    up_order = (2 + c, 3 - c, c, 1 - c)
    down_order = (c, 1 - c, 2 + c, 3 - c)
    gather_order = (c, 1 - c, 2 + c, 3 - c)

    def block_cols(b):
        return lax.div(b, 2), pl.ds(2 * lax.rem(b, 2), 2)

    def weight_block(b):
        row, cols = block_cols(b)
        return wf[row, cols].reshape(ROWS, ROWS)

    def partial(u, b):
        value = dot(att[...], weight_block(b), NT)
        for r in range(4):
            pb[u, r] = value[:, r * 128 : (r + 1) * 128]

    def reduce_copy(u, idx):
        src, dst = (su, ru) if u == 0 else (sd, rd)
        return remote(
            src.at[idx], dst.at[idx], z_send.at[u], rs_recv.at[u, idx], head=up if u == 0 else down
        )

    def reduce_send(u, idx, r, received):
        src, dst = (su, ru) if u == 0 else (sd, rd)
        value = pb[u, r]
        if received is not None:
            reduce_copy(u, received).wait_recv()
            value = value + dst[received].astype(F32)
        src[idx] = value.astype(BF16)
        reduce_copy(u, idx).start()

    row4, cols4 = block_cols(block(4))
    for i, core in enumerate((c, sibling)):
        if i == 1:
            weight_ready(4)
        value = dot(att[...], wf[row4, cols4, core].reshape(256, ROWS), NT)
        su[i] = value[:, 0:128].astype(BF16)
        sd[i] = value[:, 128:256].astype(BF16)
        reduce_copy(0, i).start()
        reduce_copy(1, i).start()
    weight_2(3)
    weight_3(3)
    weight_1(2)

    @pl.when(level_row(1) == y)
    def _():
        weight_y(1)

    weight_ready(3)
    partial(0, block(3))
    partial(1, block(-3))
    for j in range(4):
        reduce_send(0, 2 + j, up_order[j], None if j < 2 else j - 2)
        reduce_send(1, 2 + j, down_order[j], None if j < 2 else j - 2)
    for k in (2, 1):
        weight_2(k)
        weight_3(k)
        weight_ready(k)
        if k == 2:
            weight_1(1)
        partial(0, block(k))
        partial(1, block(-k))
        for j in range(4):
            idx = 4 * (3 - k) + 2 + j
            reduce_send(0, idx, up_order[j], idx - 4)
            reduce_send(1, idx, down_order[j], idx - 4)
    partial(0, z)

    def gather_copy(u, idx, b, r):
        return remote(
            res.at[b, r], res.at[b, r], z_send.at[2 + u], ag_recv.at[u, idx], head=up if u == 0 else down
        )

    loads[4].wait()
    for j, r in enumerate(gather_order):
        i_up = 10 + (2, 3, 0, 1)[j]
        i_down = 10 + j
        reduce_copy(0, i_up).wait_recv()
        reduce_copy(1, i_down).wait_recv()
        value = (pb[0, r] + ru[i_up].astype(F32) + rd[i_down].astype(F32)).astype(BF16)
        cols = pl.ds(pl.multiple_of(r * 128, 128), 128)
        ov[:, cols] = value
        res[z, r] = (value.astype(F32) - tb[:, cols].astype(F32)).astype(BF16)
        gather_copy(0, j, z, r).start()
        gather_copy(1, j, z, r).start()
    out_copy = pltpu.make_async_copy(ov, out_o, out_sem.at[0])
    out_copy.start()

    def residual_block(b, pieces):
        return jnp.concatenate([res[b, r] for r in pieces], axis=1)

    def grads(b, begin=False):
        term = dot(residual_block(b, range(4)), weight_block(b), NN)
        da[...] = term if begin else da[...] + term

    def weight_grads(b):
        row, cols = block_cols(b)
        d_b = dot(residual_block(b, range(4)), att[...], TN).astype(BF16)
        dw[row, cols] = d_b.reshape(2, 2, 128, ROWS)

    def dw_to_core(row, cols, level, slot):
        return remote(
            dw.at[row, cols, sibling], cw.at[level - 1, cols], d_send.at[0], dc_recv.at[slot], seq_2=sibling
        )

    every = pl.ds(0, 4)

    def dw_side(level, toward_right, whole):
        to = right if toward_right else left
        side = 0 if toward_right else 1
        sem = dx_recv.at[4 * (level - 1) + side + (0 if whole else 2)]
        if whole:
            return remote(xs.at[level - 1, to], xr.at[level - 1, side], d_send.at[1], sem, seq_1=to)
        part = first_half if toward_right else second_half
        return remote(
            xs.at[level - 1, across, part], xh.at[level - 1, side], d_send.at[1], sem, seq_1=to
        )

    def dw_1(level):
        row = level_row(level)
        dw_to_core(row, every, level, level - 1).wait_recv()
        for i, to in enumerate((across, right, left, x)):
            xs[level - 1, to] = (
                dw[row, to, c].astype(F32) + cw[level - 1, to].astype(F32)
            ).astype(BF16)
            if i == 0:
                dw_side(level, True, False).start()
                dw_side(level, False, False).start()

    def dw_2(level):
        for side, toward_right in enumerate((True, False)):
            to = right if toward_right else left
            part = first_half if toward_right else second_half
            dw_side(level, toward_right, False).wait_recv()
            value = xs[level - 1, to, part].astype(F32) + xh[level - 1, side].astype(F32)
            xs[level - 1, to, part] = value.astype(BF16)
            dw_side(level, toward_right, True).start()

    def dw_3(level):
        row = level_row(level)
        total = xs[level - 1, x].astype(F32)
        for side, toward_right in enumerate((True, False)):
            dw_side(level, toward_right, True).wait_recv()
            total = total + xr[level - 1, side].astype(F32)

        @pl.when(row == y)
        def _():
            yown[...] = total

        @pl.when(row != y)
        def _():
            ysend[level - 1] = total.astype(BF16)
            d = lax.rem(row - y + 4, 4)
            remote(
                ysend.at[level - 1], yrecv.at[d - 1], d_send.at[2], dy_recv.at[d - 1], seq_0=row
            ).start()

    first_col = 2 * lax.rem(block(4), 2)
    other_col = 2 - first_col
    row3 = level_row(3)
    piece_cols = (
        first_col, first_col + 1, other_col, other_col, other_col + 1, other_col + 1, first_col, first_col + 1
    )
    piece_rows = (row3, row3, row3, row4, row3, row4, row4, row4)
    piece_group = (2, 2, 2, 3, 2, 3, 3, 3)

    def lanes(q):
        return pl.ds(pl.multiple_of(q * 128, 128), 128)

    def along(x_axis, to):
        return {"seq_1": to} if x_axis else {"seq_0": to}

    def piece_to_core(p, count=1):
        cols = pl.ds(piece_cols[p], count)
        return remote(
            dw.at[piece_rows[p], cols, sibling], cw.at[piece_group[p], cols], d_send.at[0],
            dc_recv.at[2 + p], seq_2=sibling,
        )

    def quarter_copy(p, d):
        x_axis = p < 6
        to = lax.rem((x if x_axis else y) + d, 4)
        return remote(
            xs.at[piece_group[p], piece_cols[p], :, lanes(to)], h1.at[p, d - 1], d_send.at[3],
            q1_recv.at[p, d - 1], **along(x_axis, to),
        )

    def quarter_place(p):
        to_col = lax.rem(piece_cols[p] - x + 4, 4)
        to_row = lax.rem(piece_rows[p] - y + 4, 4)
        return (to_row, to_col) if p < 6 else (to_col, to_row)

    def quarter_1(p):
        row, col, group = piece_rows[p], piece_cols[p], piece_group[p]
        if p == 0:
            piece_to_core(0, 2).wait_recv()
        elif p != 1:
            piece_to_core(p).wait_recv()
        xs[group, col] = (dw[row, col, c].astype(F32) + cw[group, col].astype(F32)).astype(BF16)
        for d in (2, 1, 3):
            quarter_copy(p, d).start()

    def quarter_2(p):
        total = xs[piece_group[p], piece_cols[p], :, lanes(x if p < 6 else y)].astype(F32)
        for d in (1, 3, 2):
            quarter_copy(p, d).wait_recv()
            total = total + h1[p, d - 1].astype(F32)
        away, _ = quarter_place(p)
        hk[p] = total

        @pl.when(away != 0)
        def _():
            h2[p] = total.astype(BF16)
            to = piece_rows[p] if p < 6 else piece_cols[p]
            remote(
                h2.at[p], h2r.at[p, away - 1], q2_send.at[p], q2_recv.at[p, away - 1], **along(p >= 6, to)
            ).start()

    def quarter_3(p):
        away, rest = quarter_place(p)

        @pl.when(away == 0)
        def _():
            total = hk[p]
            for d in (1, 3, 2):
                remote(
                    h2r.at[p, d - 1], h2r.at[p, d - 1], q2_send.at[p], q2_recv.at[p, d - 1],
                    **along(p >= 6, lax.rem((x if p >= 6 else y) + d, 4)),
                ).wait_recv()
                total = total + h2r[p, d - 1].astype(F32)

            @pl.when(rest == 0)
            def _():
                yown[:, lanes(x if p < 6 else y)] = total

            @pl.when(rest != 0)
            def _():
                h3[p] = total.astype(BF16)
                group = 0 if p < 6 else 1
                to = piece_cols[p] if p < 6 else piece_rows[p]
                remote(
                    h3.at[p], h3r.at[group, rest - 1], q3_send.at[p], q3_recv.at[group, rest - 1],
                    **along(p < 6, to),
                ).start()

    def quarter_end(group):
        axis_place = x if group == 0 else y
        for d in (1, 3, 2):
            remote(
                h3r.at[group, d - 1], h3r.at[group, d - 1], q3_send.at[0], q3_recv.at[group, d - 1],
                **along(group == 0, lax.rem(axis_place + d, 4)),
            ).wait_recv()
            yown[:, lanes(lax.rem(axis_place - d + 4, 4))] = h3r[group, d - 1].astype(F32)

    grads(z, begin=True)
    weight_grads(z)
    def half_block(b, i):
        row, cols = block_cols(b)
        col = 2 * lax.rem(b, 2) + i
        pieces = residual_block(b, (2 * i, 2 * i + 1))
        d_b = dot(pieces, att[...], TN).astype(BF16)
        dw[row, col] = d_b.reshape(2, 128, ROWS)
        return dot(pieces, wf[row, col].reshape(256, ROWS), NN)

    def both_halves(i):
        @pl.loop(0, 2)
        def _(u):
            da[...] += half_block(block(3 * (2 * u - 1)), i)

    def chunk(k, j):
        r = gather_order[j]
        for u in (0, 1):
            b = block(-k if u == 0 else k)
            gather_copy(u, 4 * (k - 1) + j, b, r).wait_recv()
            if k < 3:
                gather_copy(u, 4 * k + j, b, r).start()
            elif j % 2 == u:
                gather_copy(u, 12 + j // 2, b, r).start()

    for k in (1, 2):
        for j in range(4):
            chunk(k, j)
            if k == 2 and j == 0:
                dw_1(1)
            if k == 2 and j == 2:
                dw_2(1)

        @pl.loop(0, 2)
        def _(u, k=k):
            b = block(k * (2 * u - 1))
            grads(b)
            weight_grads(b)

        dw_to_core(level_row(k), every, k, k - 1).start()
    piece_to_core(0, 2).start()
    chunk(3, 0)
    dw_1(2)
    quarter_1(0)
    quarter_1(1)
    chunk(3, 1)
    both_halves(0)
    piece_to_core(2).start()
    piece_to_core(3).start()
    dw_3(1)
    chunk(3, 2)
    dw_2(2)
    quarter_1(2)
    quarter_1(3)
    quarter_2(0)
    quarter_2(1)
    chunk(3, 3)
    both_halves(1)
    piece_to_core(4).start()
    piece_to_core(5).start()

    b4 = block(4)

    def last_half(i):
        gather_copy(0, 12 + i, b4, gather_order[2 * i]).wait_recv()
        gather_copy(1, 12 + i, b4, gather_order[2 * i + 1]).wait_recv()
        term = dot(residual_block(b4, (2 * i, 2 * i + 1)), wf[row4, first_col + i].reshape(256, ROWS), NN)
        if i == 0:
            da[...] += term
        else:
            dab[...] = (da[...] + term).astype(BF16)

    def last_weight_half(i):
        d_b = dot(residual_block(b4, (2 * i, 2 * i + 1)), att[...], TN).astype(BF16)
        dw[row4, first_col + i] = d_b.reshape(2, 128, ROWS)
        piece_to_core(6 + i).start()

    last_half(0)
    last_weight_half(0)
    quarter_1(4)
    quarter_1(5)
    dw_3(2)
    last_half(1)

    for h in range(HEADS):
        cols = head_columns(h)
        tot[1, h] = dot(scaled[:, cols], dab[:, cols], TN)

    scan_begin(1)
    last_weight_half(1)
    quarter_2(2)
    quarter_2(3)
    scan_x(1)
    quarter_1(6)
    quarter_1(7)
    quarter_3(0)
    quarter_3(1)

    def gradient_pair(start):
        for h in (start, start + 1):
            cols = head_columns(h)
            mixed = jnp.where(causal, dot(dab[:, cols], vb[:, cols], NT), 0.0).astype(BF16)
            g = dot(dab[:, cols], state[0, h], NT) + dot(mixed, kb[:, cols], NN)
            oq[:, cols] = (g * scale).astype(BF16)
            gk_acc[:, cols] = dot(mixed, scaled[:, cols], TN)
            gv_acc[:, cols] = dot(scores[h], dab[:, cols], TN)

    gradient_pair(0)
    quarter_2(4)
    quarter_2(5)
    quarter_3(2)
    quarter_3(3)
    gradient_pair(2)
    scan_y(1, True)
    q_copy = pltpu.make_async_copy(oq, gq_o, out_sem.at[1])
    q_copy.start()
    quarter_2(6)
    quarter_2(7)
    quarter_3(4)
    quarter_3(5)
    scan_core(1, True)
    quarter_3(6)
    quarter_3(7)
    scan_end(1, True)
    out_copy.wait()

    for h in range(HEADS):
        cols = head_columns(h)
        ok[:, cols] = (gk_acc[:, cols] + dot(vb[:, cols], state[1, h], NT)).astype(BF16)

    k_copy = pltpu.make_async_copy(ok, gk_o, out_sem.at[2])
    k_copy.start()

    for h in range(HEADS):
        cols = head_columns(h)
        ov[:, cols] = (gv_acc[:, cols] + dot(kb[:, cols], state[1, h], NN)).astype(BF16)

    v_copy = pltpu.make_async_copy(ov, gv_o, out_sem.at[3])
    v_copy.start()

    in_last = jnp.logical_or(row3 == y, row4 == y)

    @pl.when(jnp.logical_not(in_last))
    def _():
        total = yown[...]
        for d in (1, 3, 2):
            remote(
                yrecv.at[d - 1], yrecv.at[d - 1], d_send.at[2], dy_recv.at[d - 1], seq_0=lax.rem(y + d, 4)
            ).wait_recv()
            total = total + yrecv[d - 1].astype(F32)
        yown[...] = total

    in_second = jnp.logical_and(row4 == y, lax.div(x, 2) == lax.div(first_col, 2))

    @pl.when(jnp.logical_and(in_last, jnp.logical_not(in_second)))
    def _():
        quarter_end(0)

    @pl.when(in_second)
    def _():
        quarter_end(1)

    yown[...] = yown[...] * weight_factor
    w_copy = pltpu.make_async_copy(yown, gw_o, out_sem.at[4])
    w_copy.start()

    wait_bytes(su, z_send.at[0])
    wait_bytes(sd, z_send.at[1])
    wait_bytes(su, z_send.at[2])
    wait_bytes(sd, z_send.at[3])
    wait_bytes(yrecv, w_send.at[0])
    wait_bytes(su.at[pl.ds(0, 12)], w_send.at[1])
    wait_bytes(xs, w_send.at[2])
    wait_bytes(cw, d_send.at[0])
    wait_bytes(su.at[pl.ds(0, 6)], d_send.at[1])

    @pl.when(in_last)
    def _():
        wait_bytes(yrecv.at[pl.ds(0, 2)], d_send.at[2])

    @pl.when(jnp.logical_not(in_last))
    def _():
        wait_bytes(yrecv.at[0], d_send.at[2])

    wait_bytes(su.at[pl.ds(0, 6)], d_send.at[3])
    for p in range(8):
        away, rest = quarter_place(p)

        @pl.when(away != 0)
        def _(p=p):
            wait_bytes(h2.at[p], q2_send.at[p])

        @pl.when(jnp.logical_and(away == 0, rest != 0))
        def _(p=p):
            wait_bytes(h3.at[p], q3_send.at[p])

    for n in (0, 1):
        wait_bytes(loc.at[n], sc_send.at[n, 0])
        wait_bytes(xrc.at[n], sc_send.at[n, 1])
        wait_bytes(yrc.at[n], sc_send.at[n, 2])
        wait_bytes(pfs.at[n], sc_send.at[n, 3])
    for copy in (q_copy, k_copy, v_copy, w_copy):
        copy.wait()


def write_out(*refs):
    sems = refs[-1]
    copies = [pltpu.make_async_copy(refs[i], refs[5 + i], sems.at[i]) for i in range(5)]
    for copy in copies:
        copy.start()
    for copy in copies:
        copy.wait()


def on_device(query_rows, key_rows, value_rows, out_weight, target_rows):
    rows = jax.ShapeDtypeStruct((ROWS, ROWS), BF16)
    total_rows = query_rows.shape[0] * lax.axis_size(SEQ)
    full = (ROWS, ROWS)
    vm = pltpu.VMEM
    scratch = (
        [vm(full, BF16)] * 5
        + [
            vm((4, 4, 2, 128, ROWS), BF16),
            vm(full, BF16),
            vm((2, 4, ROWS, 128), F32),
        ]
        + [vm((14, ROWS, 128), BF16)] * 4
        + [
            vm((8, 4, ROWS, 128), BF16),
            vm(full, F32),
            vm(full, BF16),
            vm((4, 4, 2, 128, ROWS), BF16),
            vm((4, 4, 128, ROWS), BF16),
            vm((4, 4, 128, ROWS), BF16),
            vm((4, 2, 64, ROWS), BF16),
            vm((4, 2, 128, ROWS), BF16),
            vm((4, 128, ROWS), BF16),
            vm((128, ROWS), F32),
            vm((3, 128, ROWS), BF16),
            vm((HEADS, ROWS, ROWS), BF16),
            vm(full, F32),
            vm(full, F32),
        ]
        + [vm(full, BF16)] * 3
        + [
            vm((2, HEADS, DH, DH), F32),
            vm((2, HEADS, DH, DH), BF16),
            vm((2, HEADS, DH, DH), BF16),
            vm((2, 2, DH, DH), BF16),
            vm((2, 3, 2, DH, DH), BF16),
            vm((2, 2, DH, DH), BF16),
            vm((2, 3, 2, DH, DH), BF16),
            vm((2, 2, DH, DH), BF16),
            vm((2, 2, DH, DH), BF16),
            vm((2, 2, DH, DH), F32),
            vm((2, HEADS, DH, DH), BF16),
            vm((8, 3, 128, 128), BF16),
            vm((8, 128, 128), BF16),
            vm((8, 3, 128, 128), BF16),
            vm((8, 128, 128), F32),
            vm((8, 128, 128), BF16),
            vm((2, 3, 128, 128), BF16),
        ]
    )
    dma = pltpu.SemaphoreType.DMA
    scratch += [
        dma((5,)), dma((5,)), dma((2, 14)), dma((2, 14)), dma((4,)), dma((6,)), dma((24,)), dma((16,)),
        dma((3,)), dma((2, 15)), dma((2, 4)), dma((10,)), dma((8,)), dma((3,)), dma((4,)),
        dma((8, 3)), dma((8, 3)), dma((8,)), dma((2, 3)), dma((8,)),
    ]
    anywhere = pl.BlockSpec(memory_space=pl.ANY)

    arguments = (query_rows, key_rows, value_rows, out_weight, target_rows)

    def body(*refs):
        kernel(1.0 / math.sqrt(total_rows), *refs)

    shapes = (rows, rows, rows, rows, jax.ShapeDtypeStruct((128, ROWS), F32))
    results = pl.pallas_call(
        body,
        out_shape=shapes,
        in_specs=[pl.BlockSpec(memory_space=pltpu.HBM)] * 5,
        out_specs=(anywhere,) * 5,
        scratch_shapes=scratch,
        compiler_params=pltpu.CompilerParams(
            collective_id=0, has_side_effects=True, vmem_limit_bytes=48 * 1024 * 1024
        ),
        name="linear_attention",
    )(*(pltpu.with_memory_space_constraint(a, pltpu.HBM) for a in arguments))
    return pl.pallas_call(
        write_out,
        out_shape=shapes,
        in_specs=[anywhere] * 5,
        out_specs=(pl.BlockSpec(memory_space=pltpu.HBM),) * 5,
        scratch_shapes=[dma((5,))],
        compiler_params=pltpu.CompilerParams(vmem_limit_bytes=1024 * 1024),
        name="write_out",
    )(*results)


def solution(mesh):
    torus = Mesh(
        mesh.devices.reshape(4, 4, 2, mesh.shape["head"]), ("seq_0", "seq_1", "seq_2", "head")
    )
    spec = P(SEQ, "head")
    return jax.shard_map(
        on_device, mesh=torus, in_specs=(spec,) * 5, out_specs=(spec,) * 5, check_vma=False
    )
```
